32 devices in a mesh: dp: 16 (over z, y, x), fsdp: 2 (over core).
Axes of the slice: x: 2, y: 2, z: 4, core: 2. Of those that a mesh axis runs over, the one named last changes fastest.
Arguments:
- token_ids: int32 [64, 512], P(('dp', 'fsdp')), may hold values from 0 to 250111, as said below
- seq_lengths: int32 [64], P(('dp', 'fsdp')), may hold values from 128 to 512, as said below
- embedding: float32 [250112, 768], P('dp', 'fsdp'), may hold values from -6 to 6
- embed_rows: float32 [250112], replicated, may hold values from 1e-08 to 2e-06
- embed_cols: float32 [768], replicated, may hold values from 2e-08 to 4e-07
- layers: float32 [1, 768, 9216], P(None, 'dp', 'fsdp'), may hold values from -6 to 6
- layer_rows: float32 [1, 6, 768], replicated, may hold values from 0.0001 to 0.1
- layer_cols: float32 [1, 9216], replicated, may hold values from 0.0001 to 0.1
- head_weight: float32 [768, 768], replicated, may hold values from -0.21875 to 0.21875
- head_rows: float32 [768], replicated, may hold values from 0.0001 to 0.1
- head_cols: float32 [768], replicated, may hold values from 0.0001 to 0.1
- positions: float32 [512, 768], replicated, may hold values from -3 to 3
- pos_rows: float32 [512], replicated, may hold values from 2e-06 to 0.0001
- pos_cols: float32 [768], replicated, may hold values from 2e-06 to 0.0001
- norm_vectors: float32 [14, 768], replicated, may hold values from -1 to 2
- vector_moment: float32 [14, 768], replicated, may hold values from 0.0001 to 0.1
- log_scale: float32 [], replicated, may hold values from 3.4 to 4
- scale_moment: float32 [], replicated, may hold values from 0.01 to 1
Outputs:
- contrast_loss: float32 [], replicated
- embedding_new: float32 [250112, 768], P('dp', 'fsdp')
- embed_rows_new: float32 [250112], replicated
- embed_cols_new: float32 [768], replicated
- embedding_copy: bfloat16 [250112, 768], P('dp', 'fsdp')
- layers_new: float32 [1, 768, 9216], P(None, 'dp', 'fsdp')
- layer_rows_new: float32 [1, 6, 768], replicated
- layer_cols_new: float32 [1, 9216], replicated
- layers_copy: bfloat16 [1, 768, 9216], P(None, 'dp', 'fsdp')
- head_new: float32 [768, 768], replicated
- head_rows_new: float32 [768], replicated
- head_cols_new: float32 [768], replicated
- positions_new: float32 [512, 768], replicated
- pos_rows_new: float32 [512], replicated
- pos_cols_new: float32 [768], replicated
- vectors_new: float32 [14, 768], replicated
- vector_moment_new: float32 [14, 768], replicated
- log_scale_new: float32 [], replicated
- scale_moment_new: float32 [], replicated
- update_rms: float32 [11], replicated
The draws below stay inside these ranges and needn't reach their ends.
Inputs may be any that keep to these rules, and one draw needn't show every extreme that they name: `token_ids`: in the 2 sequences of each device (aligned blocks of 2 rows), exactly 64 of the 2 x 512 slots hold tokens of each run of 15632 consecutive vocabulary rows. `seq_lengths`: some sequence has exactly 512 tokens.
All inputs are finite; a program needn't handle non-finite values.
Results may differ from the reference program's by a relative error of at most 0.0025.
The reference program's roundings to bfloat16 on the way count: a program that leaves them out, or rounds other values in their place, can miss the bound.
Values may be sent and summed in bfloat16 or wider, within the bound.
No kernel may reach another device: no remote copies, remote signals or barrier semaphores. Data moves between devices by JAX's collectives and lax.ppermute only.
A program may use at most 320 MiB of HBM per device.

```python
import math
import jax
import jax.numpy as jnp
from jax import lax

MODEL_WIDTH = 768
HEADS = 12
HEAD = 64
FF = 3072
VOCAB = 250112
LAYERS = 1
MAXLEN = 512
MINLEN = 128
SEQ_DEV = 2
SEQS = 64
VOC_SHARD = 15632
CAPS = 64
COLS = 9216
GROWS = 14


def draw_token_ids(key, part):
    key_owner, key_one, key_two = jax.random.split(key, 3)
    block_count = SEQS // SEQ_DEV
    slot_count = SEQ_DEV * MAXLEN
    owner_base = jnp.arange(slot_count, dtype=jnp.int32) // CAPS
    owners = jax.vmap(lambda subkey: jax.random.permutation(subkey, owner_base))(jax.random.split(key_owner, block_count))
    draw_one = jax.random.randint(key_one, (block_count, slot_count), 0, VOC_SHARD)
    second = jax.random.randint(key_two, (block_count, slot_count), 0, VOC_SHARD)
    offsets = jnp.minimum(draw_one, second)
    return (owners * VOC_SHARD + offsets).reshape(SEQS, MAXLEN).astype(jnp.int32)


def draw_seq_lengths(key, part):
    key_length, key_pick = jax.random.split(key)
    lengths = jax.random.randint(key_length, (SEQS,), MINLEN, MAXLEN + 1)
    chosen = jax.random.randint(key_pick, (), 0, SEQS)
    return jnp.where(jnp.arange(SEQS) == chosen, MAXLEN, lengths).astype(jnp.int32)


def draw_layers(key, part):
    width = 4 * MODEL_WIDTH + 2 * FF
    noise = jnp.clip(jax.random.normal(key, (LAYERS, MODEL_WIDTH, width), jnp.float32), -6.0, 6.0)
    column = jnp.arange(width)
    scaling = jnp.where(column < 3 * MODEL_WIDTH, MODEL_WIDTH ** (-0.5), jnp.where(column < 4 * MODEL_WIDTH, 4.0 * MODEL_WIDTH ** (-0.5), jnp.where(column < 4 * MODEL_WIDTH + FF, MODEL_WIDTH ** (-0.5), FF ** (-0.5))))
    return (noise * scaling[None, None, :]).astype(jnp.float32)


def draw_norm_vectors(key, part):
    per_layer = 8 + FF // MODEL_WIDTH
    row_total = 2 + LAYERS * per_layer
    noise = jnp.clip(jax.random.normal(key, (row_total, MODEL_WIDTH), jnp.float32), -4.0, 4.0)
    index = jnp.arange(row_total)
    within = (index - 2) % per_layer
    is_gain = (index == 0) | (index >= 2) & ((within == 4) | (within == 6))
    return jnp.where(is_gain[:, None], 1.0 + 0.1 * noise, 0.05 * noise).astype(jnp.float32)


def levels(own_key, dims, shards, smallest, top_value):
    def one(dim, parts):
        draws = jax.random.uniform(jax.random.fold_in(jax.random.fold_in(own_key, 6), dim), (parts,), jnp.float32, smallest / len(shards), top_value / len(shards))
        return jnp.repeat(jnp.exp(draws), dims[dim] // parts).reshape((-1,) + (1,) * (len(dims) - dim - 1))

    loudness = one(*shards[0])
    for cut in shards[1:]:
        loudness = loudness * one(*cut)
    return loudness


def centred(key, dims, scale, reach, cuts=(), kind=jnp.bfloat16):
    gain = levels(key, dims, cuts, -0.22, 0.18) if cuts else 1.0
    result = jax.random.normal(key, dims, jnp.float32) * scale * gain
    return jnp.minimum(jnp.maximum(result, -reach), reach).astype(kind)


def setup_inputs(seed: int = 0) -> dict:
    key_list = jax.random.split(jax.random.key(seed), 19)
    token_ids = draw_token_ids(jax.random.fold_in(key_list[18], 71), 0)
    seq_lengths = draw_seq_lengths(jax.random.fold_in(key_list[18], 71), 0)
    embedding = centred(key_list[2], (VOCAB, MODEL_WIDTH), 1.0, 6.0, ((0, 16), (1, 2)), jnp.float32)
    embed_rows = jnp.clip(jnp.exp(jax.random.uniform(key_list[3], (VOCAB,), jnp.float32, math.log(9.99999993922529e-09), math.log(1.9999999949504854e-06))), 9.99999993922529e-09, 1.9999999949504854e-06)
    embed_cols = jnp.clip(jnp.exp(jax.random.uniform(key_list[4], (MODEL_WIDTH,), jnp.float32, math.log(1.999999987845058e-08), math.log(4.0000000467443897e-07))), 1.999999987845058e-08, 4.0000000467443897e-07)
    layers = draw_layers(jax.random.fold_in(key_list[18], 71), 0)
    layer_rows = jnp.clip(jnp.exp(jax.random.uniform(key_list[6], (LAYERS, 6, MODEL_WIDTH), jnp.float32, math.log(0.0001), math.log(0.1))), 0.0001, 0.1)
    layer_cols = jnp.clip(jnp.exp(jax.random.uniform(key_list[7], (LAYERS, COLS), jnp.float32, math.log(0.0001), math.log(0.1))), 0.0001, 0.1)
    head_weight = centred(key_list[8], (MODEL_WIDTH, MODEL_WIDTH), MODEL_WIDTH ** -0.5, 0.21875, (), jnp.float32)
    head_rows = jnp.clip(jnp.exp(jax.random.uniform(key_list[9], (MODEL_WIDTH,), jnp.float32, math.log(0.0001), math.log(0.1))), 0.0001, 0.1)
    head_cols = jnp.clip(jnp.exp(jax.random.uniform(key_list[10], (MODEL_WIDTH,), jnp.float32, math.log(0.0001), math.log(0.1))), 0.0001, 0.1)
    positions = centred(key_list[11], (MAXLEN, MODEL_WIDTH), 0.5, 3.0, (), jnp.float32)
    pos_rows = jnp.clip(jnp.exp(jax.random.uniform(key_list[12], (MAXLEN,), jnp.float32, math.log(1.9999999949504854e-06), math.log(0.0001))), 1.9999999949504854e-06, 0.0001)
    pos_cols = jnp.clip(jnp.exp(jax.random.uniform(key_list[13], (MODEL_WIDTH,), jnp.float32, math.log(1.9999999949504854e-06), math.log(0.0001))), 1.9999999949504854e-06, 0.0001)
    norm_vectors = draw_norm_vectors(jax.random.fold_in(key_list[18], 71), 0)
    vector_moment = jnp.clip(jnp.exp(jax.random.uniform(key_list[15], (GROWS, MODEL_WIDTH), jnp.float32, math.log(0.0001), math.log(0.1))), 0.0001, 0.1)
    log_scale = jnp.clip(jax.random.uniform(key_list[16], (), jnp.float32, 3.4, 4.0), 3.4, 4.0)
    scale_moment = jnp.clip(jnp.exp(jax.random.uniform(key_list[17], (), jnp.float32, math.log(0.01), math.log(1.0))), 0.01, 1.0)
    return {"token_ids": token_ids, "seq_lengths": seq_lengths, "embedding": embedding, "embed_rows": embed_rows, "embed_cols": embed_cols, "layers": layers, "layer_rows": layer_rows, "layer_cols": layer_cols, "head_weight": head_weight, "head_rows": head_rows, "head_cols": head_cols, "positions": positions, "pos_rows": pos_rows, "pos_cols": pos_cols, "norm_vectors": norm_vectors, "vector_moment": vector_moment, "log_scale": log_scale, "scale_moment": scale_moment}


NORM_EPSILON = 1e-05
UNIT_EPSILON = 1e-06
DECAY_RATE = 0.5
FLOOR_SQUARE = 1e-30
FLOOR_SCALE = 0.001
CLIP_LIMIT = 1.0
RELATIVE = 0.3
EXACT_PRECISION = lax.Precision.HIGHEST

@jax.custom_vjp
def low(v):
    return lax.optimization_barrier(v.astype(jnp.bfloat16)).astype(jnp.float32)

@jax.custom_vjp
def reduced_gradient(v):
    return v

def low_keep(v):
    return (low(v), None)

def low_pass(kept, grad):
    return (grad,)

def back_keep(v):
    return (v, None)

def back_low(kept, grad):
    return (low(grad),)
low.defvjp(low_keep, low_pass)
reduced_gradient.defvjp(back_keep, back_low)

def layer_norm(values, gain_row, bias_row):
    center = values - lax.optimization_barrier(jnp.mean(values, -1, keepdims=True))
    spread = lax.optimization_barrier(jnp.mean(center * center, -1, keepdims=True))
    return center * lax.rsqrt(spread + NORM_EPSILON) * gain_row + bias_row

def gelu_exact(values):
    return jax.nn.gelu(values, approximate=False)

def project(pooled, head_weight):
    projected = jnp.dot(pooled, head_weight, precision=EXACT_PRECISION)
    return projected * lax.rsqrt(lax.optimization_barrier(jnp.sum(projected * projected, -1, keepdims=True)) + UNIT_EPSILON)

def log_total(logits, reduce_axis):
    row_peak = lax.optimization_barrier(jnp.max(logits, reduce_axis, keepdims=True))
    return jnp.squeeze(row_peak, reduce_axis) + jnp.log(lax.optimization_barrier(jnp.sum(jnp.exp(logits - row_peak), reduce_axis)))

def contrast(unit_rows, log_scale):
    first_view = unit_rows[0::2]
    second_view = unit_rows[1::2]
    logits = jnp.exp(log_scale) * jnp.dot(first_view, second_view.T, precision=EXACT_PRECISION)
    matched = jnp.diagonal(logits)
    return 0.5 * (jnp.sum(log_total(logits, 1) - matched) + jnp.sum(log_total(logits, 0) - matched))

def factored_step(gradient, rows_old, cols_old):
    square = gradient * gradient
    rows_new = DECAY_RATE * rows_old + (1.0 - DECAY_RATE) * (lax.optimization_barrier(jnp.mean(square, 1)) + FLOOR_SQUARE)
    cols_new = DECAY_RATE * cols_old + (1.0 - DECAY_RATE) * (lax.optimization_barrier(jnp.mean(square, 0)) + FLOOR_SQUARE)
    estimate = rows_new[:, None] * cols_new[None, :] / jnp.mean(rows_new)
    return (gradient * lax.rsqrt(estimate), rows_new, cols_new)

def plain_step(gradient, moment_old):
    moment_new = DECAY_RATE * moment_old + (1.0 - DECAY_RATE) * (gradient * gradient + FLOOR_SQUARE)
    return (gradient * lax.rsqrt(moment_new), moment_new)

def apply_update(weight_matrix, update):
    spread = jnp.sqrt(jnp.mean(update * update))
    clip_factor = jnp.maximum(1.0, spread / CLIP_LIMIT)
    step_size = RELATIVE * jnp.maximum(FLOOR_SCALE, jnp.sqrt(jnp.mean(weight_matrix * weight_matrix)))
    return (weight_matrix - step_size * (update / clip_factor), spread)

def encoder_layer(hidden, weight_matrix, vector_params, key_valid):
    seq_count = hidden.shape[0]
    hidden_low = low(hidden)
    qkv_bias = jnp.concatenate([vector_params[0], jnp.zeros_like(vector_params[0]), vector_params[1]])
    qkv = reduced_gradient(jnp.einsum('snd,dc->snc', hidden_low, weight_matrix[:, :3 * MODEL_WIDTH], precision=EXACT_PRECISION)) + qkv_bias
    qkv = low(qkv).reshape(seq_count, MAXLEN, 3, HEADS, HEAD)
    scores = reduced_gradient(jnp.einsum('sqhe,skhe->shqk', qkv[:, :, 0], qkv[:, :, 1], precision=EXACT_PRECISION) * 0.125)
    scores = jnp.where(key_valid[:, None, None, :], scores, -1e+30)
    row_peak = lax.optimization_barrier(jnp.max(scores, -1, keepdims=True))
    raised = jnp.exp(scores - row_peak)
    soft_weights = low(raised / lax.optimization_barrier(jnp.sum(raised, -1, keepdims=True)))
    attention_output = jnp.einsum('shqk,skhe->sqhe', soft_weights, qkv[:, :, 2], precision=EXACT_PRECISION).reshape(seq_count, MAXLEN, MODEL_WIDTH)
    attention_output = low(reduced_gradient(attention_output))
    result_output = reduced_gradient(jnp.einsum('xui,iv->xuv', attention_output, weight_matrix[:, 3 * MODEL_WIDTH:4 * MODEL_WIDTH], precision=EXACT_PRECISION)) + vector_params[2]
    first_norm = layer_norm(hidden + result_output, vector_params[4], vector_params[5])
    upward = reduced_gradient(jnp.einsum('snd,df->snf', low(first_norm), weight_matrix[:, 4 * MODEL_WIDTH:4 * MODEL_WIDTH + FF], precision=EXACT_PRECISION))
    upward = upward + vector_params[8:].reshape(FF)
    active = low(gelu_exact(upward))
    downward = reduced_gradient(jnp.einsum('snf,df->snd', active, weight_matrix[:, 4 * MODEL_WIDTH + FF:], precision=EXACT_PRECISION)) + vector_params[3]
    return layer_norm(first_norm + downward, vector_params[6], vector_params[7])

def encode(block_rows, lengths, weights, positions, vector_params):
    seq_count = lengths.shape[0]
    key_valid = jnp.arange(MAXLEN)[None, :] < lengths[:, None]
    hidden = layer_norm(block_rows.reshape(seq_count, MAXLEN, MODEL_WIDTH) + positions[None], vector_params[0], vector_params[1])
    per_layer = 8 + FF // MODEL_WIDTH
    for layer_index in range(LAYERS):
        first_row = 2 + layer_index * per_layer
        hidden = encoder_layer(hidden, weights[layer_index], vector_params[first_row:first_row + per_layer], key_valid)
    valid_mask = key_valid.astype(jnp.float32)
    return lax.optimization_barrier(jnp.sum(hidden * valid_mask[:, :, None], 1)) / lengths.astype(jnp.float32)[:, None]

def forward(embedding, layers, head_weight, positions, vector_params, log_scale, token_ids, seq_lengths):
    looked = reduced_gradient(low(embedding[token_ids.reshape(-1)]))
    weights = low(layers)
    group_size = math.gcd(SEQS, 8)
    group_count = SEQS // group_size
    blocks = looked.reshape(group_count, group_size * MAXLEN, MODEL_WIDTH)
    block_lengths = seq_lengths.reshape(group_count, group_size)
    encoder = jax.checkpoint(lambda block_rows, lengths: encode(block_rows, lengths, weights, positions, vector_params))
    pooled = lax.map(lambda element: encoder(element[0], element[1]), (blocks, block_lengths))
    unit_rows = project(pooled.reshape(SEQS, MODEL_WIDTH), head_weight)
    return contrast(unit_rows, log_scale)

def reference(token_ids, seq_lengths, embedding, embed_rows, embed_cols, layers, layer_rows, layer_cols, head_weight, head_rows, head_cols, positions, pos_rows, pos_cols, norm_vectors, vector_moment, log_scale, scale_moment):

    def objective(table, stacked, projection, position_table, vector_params, scale):
        return forward(table, stacked, projection, position_table, vector_params, scale, token_ids, seq_lengths)
    loss_value, pullback = jax.vjp(objective, embedding, layers, head_weight, positions, norm_vectors, log_scale)
    gradients = pullback(jnp.ones_like(loss_value))
    grad_embed, grad_layers, grad_head, grad_pos, grad_vectors, grad_scale = gradients
    embed_update, embed_rows_new, embed_cols_new = factored_step(grad_embed, embed_rows, embed_cols)
    embedding_new, embed_spread = apply_update(embedding, embed_update)
    head_update, head_rows_new, head_cols_new = factored_step(grad_head, head_rows, head_cols)
    head_new, head_spread = apply_update(head_weight, head_update)
    pos_update, pos_rows_new, pos_cols_new = factored_step(grad_pos, pos_rows, pos_cols)
    positions_new, pos_spread = apply_update(positions, pos_update)
    vector_update, vector_moment_new = plain_step(grad_vectors, vector_moment)
    vectors_new, vector_spread = apply_update(norm_vectors, vector_update)
    scale_update, scale_moment_new = plain_step(grad_scale, scale_moment)
    log_scale_new, scale_spread = apply_update(log_scale, scale_update)
    bounds = [0, MODEL_WIDTH, 2 * MODEL_WIDTH, 3 * MODEL_WIDTH, 4 * MODEL_WIDTH, 4 * MODEL_WIDTH + FF, 4 * MODEL_WIDTH + 2 * FF]
    layer_list, row_list, col_list, spreads = ([], [], [], [])
    for layer_index in range(LAYERS):
        pieces, row_pieces, col_pieces = ([], [], [])
        for block_index in range(6):
            left_col, right_col = (bounds[block_index], bounds[block_index + 1])
            update, rows_new, cols_new = factored_step(grad_layers[layer_index][:, left_col:right_col], layer_rows[layer_index, block_index], layer_cols[layer_index, left_col:right_col])
            weight_new, spread = apply_update(layers[layer_index][:, left_col:right_col], update)
            pieces.append(weight_new)
            row_pieces.append(rows_new)
            col_pieces.append(cols_new)
            spreads.append(spread)
        layer_list.append(jnp.concatenate(pieces, 1))
        row_list.append(jnp.stack(row_pieces))
        col_list.append(jnp.concatenate(col_pieces))
    layers_new = jnp.stack(layer_list)
    layer_rows_new = jnp.stack(row_list)
    layer_cols_new = jnp.stack(col_list)
    update_rms = jnp.stack([embed_spread, head_spread, pos_spread, vector_spread, scale_spread] + spreads)
    return (loss_value, embedding_new, embed_rows_new, embed_cols_new, embedding_new.astype(jnp.bfloat16), layers_new, layer_rows_new, layer_cols_new, layers_new.astype(jnp.bfloat16), head_new, head_rows_new, head_cols_new, positions_new, pos_rows_new, pos_cols_new, vectors_new, vector_moment_new, log_scale_new, scale_moment_new, update_rms)
```

```python
import functools
import math

import jax
import jax.numpy as jnp
from jax import lax
from jax.experimental import pallas as pl
from jax.experimental.pallas import tpu as pltpu
from jax.sharding import PartitionSpec as P

MODEL_WIDTH = 768
HEADS = 12
HEAD = 64
FF = 3072
VOCAB = 250112
LAYERS = 1
MAXLEN = 512
PER_LAYER = 8 + FF // MODEL_WIDTH
COLUMNS = 4 * MODEL_WIDTH + 2 * FF
PIECE = FF // 2
COLORS = 3
TILE_ROWS = 2048

NORM_EPSILON = 1e-05
UNIT_EPSILON = 1e-06
DECAY_RATE = 0.5
FLOOR_SQUARE = 1e-30
FLOOR_SCALE = 0.001
CLIP_LIMIT = 1.0
RELATIVE = 0.3
EXACT_PRECISION = lax.Precision.HIGHEST
BOTH = ("dp", "fsdp")
F32, BF16 = jnp.float32, jnp.bfloat16
CONTRACT_ROWS = (((0,), (0,)), ((), ()))
CONTRACT_COLS = (((1,), (1,)), ((), ()))
CONTRACT_IN = (((1,), (0,)), ((), ()))


def dot(left, right, dims=CONTRACT_IN):
    return lax.dot_general(left, right, dims, preferred_element_type=F32)


def bit_count(size):
    return size.bit_length() - 1


def bit_orders(size):
    count = bit_count(size)
    rest = list(range(count - 1))[::-1]
    turns = [rest[-k:] + rest[:-k] if k else rest for k in range(COLORS)]
    return [[count - 1] + turn for turn in turns]


def swap_by(values, axis, size, mask, name):
    with jax.named_scope(name):
        return lax.ppermute(values, axis, [(i, i ^ mask) for i in range(size)])


def swap(values, axis, size, bit, name):
    return swap_by(values, axis, size, 1 << bit, f"{name}_{bit}")


def own_bit(axis, bit):
    return (lax.axis_index(axis) >> bit) & 1


def gather_bits(values, axis, size, order, name):
    count = bit_count(size)
    held = values.reshape((1,) * count + values.shape)
    for bit in order:
        other = swap(held, axis, size, bit, name)
        dim = count - 1 - bit
        low_first = jnp.concatenate([held, other], dim)
        high_first = jnp.concatenate([other, held], dim)
        held = jnp.where(own_bit(axis, bit) == 0, low_first, high_first)
    return held.reshape((size,) + values.shape)


def in_order(held, size, dim):
    me = lax.axis_index("fsdp")
    for bit in range(bit_count(size)):
        mine = (me >> bit) & 1
        held = [jnp.where(mine == 0, held[k], held[k ^ (1 << bit)]) for k in range(size)]
    return jnp.concatenate(held, dim)


def gather_list(values, axis, size, name):
    held = [values] + [swap_by(values, axis, size, d, name) for d in range(1, size)]
    for bit in range(bit_count(size)):
        mine = own_bit(axis, bit)
        held = [jnp.where(mine == 0, held[k], held[k ^ (1 << bit)]) for k in range(size)]
    return held


def fsdp_others(values, size, name):
    return [swap_by(values, "fsdp", size, d, name) for d in range(1, size)]


def scatter_bits(values, axis, size, order, dim, name):
    for place, bit in enumerate(order):
        shape = values.shape
        half = shape[dim] // 2
        above = 1 << sum(1 for b in order[place + 1 :] if b > bit)
        parts = values.reshape(shape[:dim] + (above, 2, half // above) + shape[dim + 1 :])
        mine = own_bit(axis, bit)
        keep = lax.dynamic_index_in_dim(parts, mine, dim + 1, keepdims=False)
        send = lax.dynamic_index_in_dim(parts, 1 - mine, dim + 1, keepdims=False).astype(BF16)
        rest = shape[:dim] + (half,) + shape[dim + 1 :]
        values = keep.reshape(rest) + swap(send.reshape(rest), axis, size, bit, name).astype(F32)
    return values


def everyone(values, axis, size):
    return lax.all_to_all(
        jnp.broadcast_to(values[None], (size,) + values.shape), axis, 0, 0, tiled=True
    )


def padded(values, multiple):
    return jnp.pad(values, (0, -values.size % multiple))


def attention_scores(query, key_rows, length):
    scores = dot(query, key_rows, CONTRACT_COLS) * 0.125
    valid = lax.broadcasted_iota(jnp.int32, scores.shape, 1) < length
    scores = jnp.where(valid, scores, -1e30)
    raised = jnp.exp(scores - jnp.max(scores, -1, keepdims=True))
    return raised / jnp.sum(raised, -1, keepdims=True)


def attention_kernel(lengths, q_ref, k_ref, v_ref, o_ref):
    length = lengths[pl.program_id(0)]
    lanes = lax.broadcasted_iota(jnp.int32, q_ref.shape, 1)
    query, key_rows, value_rows = q_ref[...], k_ref[...], v_ref[...]
    zero = jnp.zeros_like(query)
    first = attention_scores(jnp.where(lanes < HEAD, query, zero), key_rows, length)
    second = attention_scores(jnp.where(lanes < HEAD, zero, query), key_rows, length)
    out = jnp.where(lanes < HEAD, dot(first.astype(BF16), value_rows), dot(second.astype(BF16), value_rows))
    o_ref[...] = out.astype(BF16)


def attend(lengths, qk, v):
    seqs = lengths.shape[0]
    pairs = MODEL_WIDTH // 128
    block = (MAXLEN, 128)
    return pl.pallas_call(
        attention_kernel,
        grid_spec=pltpu.PrefetchScalarGridSpec(
            num_scalar_prefetch=1,
            grid=(seqs, pairs),
            in_specs=[
                pl.BlockSpec(block, lambda s, h, n: (s, h)),
                pl.BlockSpec(block, lambda s, h, n: (s, h + pairs)),
                pl.BlockSpec(block, lambda s, h, n: (s, h)),
            ],
            out_specs=pl.BlockSpec(block, lambda s, h, n: (s, h)),
        ),
        out_shape=jax.ShapeDtypeStruct((seqs * MAXLEN, MODEL_WIDTH), BF16),
        name="attend",
    )(lengths, qk, qk, v)


def attention_back_kernel(lengths, q_ref, k_ref, v_ref, d_ref, dq_ref, dk_ref, dv_ref, sum_ref):
    length = lengths[pl.program_id(0)]
    lanes = lax.broadcasted_iota(jnp.int32, q_ref.shape, 1)
    query, key_rows, value_rows, d_rows = q_ref[...], k_ref[...], v_ref[...], d_ref[...]
    zero = jnp.zeros_like(query)
    parts = []
    for low_half in (True, False):
        take = (lanes < HEAD) if low_half else (lanes >= HEAD)
        soft = attention_scores(jnp.where(take, query, zero), key_rows, length)
        d_values = dot(soft.astype(BF16), d_rows, CONTRACT_ROWS)
        d_soft = dot(jnp.where(take, d_rows, zero), value_rows, CONTRACT_COLS)
        d_scores = soft * (d_soft - jnp.sum(soft * d_soft, -1, keepdims=True))
        d_low = d_scores.astype(BF16)
        parts.append((dot(d_low, key_rows) * 0.125, dot(d_low, query, CONTRACT_ROWS) * 0.125, d_values))
    dq, dk, dv = (jnp.where(lanes < HEAD, a, b) for a, b in zip(*parts))
    dq_ref[...] = dq.astype(BF16)
    dk_ref[...] = dk.astype(BF16)
    dv_ref[...] = dv.astype(BF16)
    sums = jnp.concatenate([jnp.sum(dq, 0, keepdims=True), jnp.sum(dv, 0, keepdims=True)], 0)
    sum_ref[...] = jnp.concatenate([sums, jnp.zeros((6, 128), F32)], 0)


def attend_back(lengths, qk, v, d_att):
    seqs = lengths.shape[0]
    pairs = MODEL_WIDTH // 128
    block = (MAXLEN, 128)
    plain = pl.BlockSpec(block, lambda s, h, n: (s, h))
    low = jax.ShapeDtypeStruct((seqs * MAXLEN, MODEL_WIDTH), BF16)
    return pl.pallas_call(
        attention_back_kernel,
        grid_spec=pltpu.PrefetchScalarGridSpec(
            num_scalar_prefetch=1,
            grid=(seqs, pairs),
            in_specs=[plain, pl.BlockSpec(block, lambda s, h, n: (s, h + pairs)), plain, plain],
            out_specs=[plain, plain, plain, pl.BlockSpec((8, 128), lambda s, h, n: (s, h))],
        ),
        out_shape=[low, low, low, jax.ShapeDtypeStruct((seqs * 8, MODEL_WIDTH), F32)],
        name="attend_back",
    )(lengths, qk, qk, v, d_att)


def rows_kernel(wanted, table_ref, out_ref, rows, sem):
    count = rows.shape[0]

    def fetch(j, carry):
        pltpu.make_async_copy(table_ref.at[pl.ds(wanted[j], 1)], rows.at[pl.ds(j, 1)], sem).start()
        return carry

    lax.fori_loop(0, count, fetch, 0, unroll=8)
    pltpu.make_async_copy(rows, rows, sem).wait()
    out_ref[...] = rows[...].astype(BF16)


def take_rows(wanted, table):
    count, width = wanted.shape[0], table.shape[1]
    return pl.pallas_call(
        rows_kernel,
        grid_spec=pltpu.PrefetchScalarGridSpec(
            num_scalar_prefetch=1,
            grid=(1,),
            in_specs=[pl.BlockSpec(memory_space=pl.ANY)],
            out_specs=pl.BlockSpec((count, width), lambda i, n: (0, 0)),
            scratch_shapes=[pltpu.VMEM((count, width), F32), pltpu.SemaphoreType.DMA],
        ),
        out_shape=jax.ShapeDtypeStruct((count, width), BF16),
        name="take_rows",
    )(wanted, table)


def table_kernel(rows_at, starts, table_ref, update_ref, scale_ref, new_ref, low_ref):
    tile = pl.program_id(0)
    base = tile * TILE_ROWS
    scale = scale_ref[...]
    new_ref[...] = table_ref[...]

    def patch(k, carry):
        row = pl.ds(rows_at[k] - base, 1)
        new_ref[row, :] = table_ref[row, :] - scale * update_ref[pl.ds(k, 1), :]
        return carry

    lax.fori_loop(starts[tile], starts[tile + 1], patch, 0)
    low_ref[...] = new_ref[...].astype(BF16)


def table_update(rows_at, starts, table, update, scale):
    height, width = table.shape
    tile = pl.BlockSpec((TILE_ROWS, width), lambda i, *_: (i, 0))
    return pl.pallas_call(
        table_kernel,
        grid_spec=pltpu.PrefetchScalarGridSpec(
            num_scalar_prefetch=2,
            grid=(pl.cdiv(height, TILE_ROWS),),
            in_specs=[
                tile,
                pl.BlockSpec(update.shape, lambda i, *_: (0, 0)),
                pl.BlockSpec(scale.shape, lambda i, *_: (0, 0)),
            ],
            out_specs=[tile, tile],
        ),
        out_shape=[
            jax.ShapeDtypeStruct((height, width), F32),
            jax.ShapeDtypeStruct((height, width), BF16),
        ],
        name="table_update",
    )(rows_at, starts, table, update, scale)


def norm_forward(values, gain_row, bias_row):
    center = values - jnp.mean(values, -1, keepdims=True)
    spread = jnp.mean(center * center, -1, keepdims=True)
    inverse = lax.rsqrt(spread + NORM_EPSILON)
    unit = center * inverse
    return unit * gain_row + bias_row, (unit, inverse)


def norm_backward(d_out, kept, gain_row):
    unit, inverse = kept
    scaled = d_out * gain_row
    d_in = inverse * (
        scaled - jnp.mean(scaled, -1, keepdims=True) - unit * jnp.mean(scaled * unit, -1, keepdims=True)
    )
    return d_in, jnp.sum(d_out * unit, 0), jnp.sum(d_out, 0)


def gelu_and_slope(values):
    normal = 0.5 + 0.5 * lax.erf(values * math.sqrt(0.5))
    slope = normal + values * (jnp.exp(-0.5 * values * values) * (1.0 / math.sqrt(2.0 * math.pi)))
    return values * normal, slope


def exact(left, right, dims=CONTRACT_IN):
    return lax.dot_general(left, right, dims, precision=EXACT_PRECISION, preferred_element_type=F32)


def contrast_kernel(scale_ref, pooled_ref, head_ref, d_pooled_ref, d_projected_ref, loss_ref):
    projected = exact(pooled_ref[...], head_ref[...])
    inverse = lax.rsqrt(jnp.sum(projected * projected, -1, keepdims=True) + UNIT_EPSILON)
    units = projected * inverse
    scale = jnp.exp(jnp.full((1, 1), scale_ref[0], F32))
    logits = scale * exact(units, units, CONTRACT_COLS)
    row = lax.broadcasted_iota(jnp.int32, logits.shape, 0)
    col = lax.broadcasted_iota(jnp.int32, logits.shape, 1)
    used = (row % 2 == 0) & (col % 2 == 1)
    pairs = used & (col == row + 1)
    total = jnp.zeros((1, 1), F32)
    d_logits = jnp.where(pairs, -1.0, 0.0)
    for axis, live in ((1, row % 2 == 0), (0, col % 2 == 1)):
        seen = jnp.where(used, logits, -1e30)
        peak = jnp.max(seen, axis, keepdims=True)
        raised = jnp.where(used, jnp.exp(seen - peak), 0.0)
        sums = jnp.sum(raised, axis, keepdims=True)
        safe = jnp.where(sums > 0.0, sums, 1.0)
        d_logits += 0.5 * raised / safe
        logs = jnp.where(sums > 0.0, peak + jnp.log(safe), 0.0)
        total += 0.5 * jnp.sum(jnp.sum(logs, 1, keepdims=True), 0, keepdims=True)
    matched = jnp.where(pairs, logits, 0.0)
    total -= jnp.sum(jnp.sum(matched, 1, keepdims=True), 0, keepdims=True)
    weighted = jnp.where(used, d_logits * logits, 0.0)
    d_scale = jnp.sum(jnp.sum(weighted, 1, keepdims=True), 0, keepdims=True)
    d_units = scale * (exact(d_logits, units) + exact(d_logits, units, CONTRACT_ROWS))
    along = jnp.sum(projected * d_units, -1, keepdims=True)
    d_projected = inverse * d_units - projected * (inverse * inverse * inverse * along)
    d_projected_ref[...] = d_projected
    d_pooled_ref[...] = exact(d_projected, head_ref[...], CONTRACT_COLS)
    lane = lax.broadcasted_iota(jnp.int32, (8, 128), 1)
    loss_ref[...] = jnp.where(lane == 0, total, jnp.where(lane == 1, d_scale, 0.0))


def contrast(pooled, head_weight, log_scale):
    vmem = pl.BlockSpec(memory_space=pltpu.VMEM)
    like = jax.ShapeDtypeStruct(pooled.shape, F32)
    return pl.pallas_call(
        contrast_kernel,
        in_specs=[pl.BlockSpec(memory_space=pltpu.SMEM), vmem, vmem],
        out_specs=[vmem] * 3,
        out_shape=[like, like, jax.ShapeDtypeStruct((8, 128), F32)],
        name="contrast",
    )(log_scale.reshape(1), pooled, head_weight)


def factored_step(gradient, rows_old, cols_old):
    square = gradient * gradient
    rows_new = DECAY_RATE * rows_old + (1.0 - DECAY_RATE) * (jnp.mean(square, 1) + FLOOR_SQUARE)
    cols_new = DECAY_RATE * cols_old + (1.0 - DECAY_RATE) * (jnp.mean(square, 0) + FLOOR_SQUARE)
    estimate = rows_new[:, None] * cols_new[None, :] / jnp.mean(rows_new)
    return (gradient * lax.rsqrt(estimate), rows_new, cols_new)


def plain_step(gradient, moment_old):
    moment_new = DECAY_RATE * moment_old + (1.0 - DECAY_RATE) * (gradient * gradient + FLOOR_SQUARE)
    return (gradient * lax.rsqrt(moment_new), moment_new)


def apply_update(weight_matrix, update):
    spread = jnp.sqrt(jnp.mean(update * update))
    clip_factor = jnp.maximum(1.0, spread / CLIP_LIMIT)
    step_size = RELATIVE * jnp.maximum(FLOOR_SCALE, jnp.sqrt(jnp.mean(weight_matrix * weight_matrix)))
    return (weight_matrix - step_size * (update / clip_factor), spread)


def body(
    token_ids,
    seq_lengths,
    embedding,
    embed_rows,
    embed_cols,
    layers,
    layer_rows,
    layer_cols,
    head_weight,
    head_rows,
    head_cols,
    positions,
    pos_rows,
    pos_cols,
    norm_vectors,
    vector_moment,
    log_scale,
    scale_moment,
):
    outer = lax.axis_size("dp")
    inner = lax.axis_size("fsdp")
    devices = outer * inner
    outer_index = lax.axis_index("dp")
    inner_index = lax.axis_index("fsdp")
    seq_count = token_ids.shape[0]
    slots = seq_count * MAXLEN
    cap = slots // outer
    shard_rows, shard_cols = embedding.shape
    local_rows, local_cols = layers.shape[1], layers.shape[2]
    gather_orders = bit_orders(outer)
    scatter_orders = [order[::-1] for order in gather_orders]
    inner_order = list(range(bit_count(inner)))

    flat = token_ids.reshape(slots)
    owners = flat // shard_rows
    offsets = flat - owners * shard_rows
    hot = owners[:, None] == jnp.arange(outer, dtype=jnp.int32)[None, :]
    counting = jnp.arange(slots, dtype=jnp.int32)
    before = dot((counting[:, None] >= counting[None, :]).astype(BF16), hot.astype(BF16))
    rank = jnp.sum(jnp.where(hot, before, 0.0), 1).astype(jnp.int32) - 1
    bucket = owners * cap + rank
    outgoing = jnp.sum(jnp.where(counting[:, None] == bucket[None, :], offsets[None, :], 0), 1)
    with jax.named_scope("ask"):
        asked = lax.all_to_all(outgoing.reshape(outer, cap), "dp", 0, 0, tiled=True)
    wanted = jnp.stack([asked] + fsdp_others(asked, inner, "ask_swap"), 1).reshape(-1)
    entries = wanted.shape[0]

    low_layers = layers[0].astype(BF16)
    width = local_cols // COLORS
    gathered = []
    for color in range(COLORS):
        piece = low_layers[:, color * width : (color + 1) * width]
        whole = gather_bits(piece, "dp", outer, gather_orders[color], f"ag{color}").reshape(MODEL_WIDTH, width)
        gathered.append(gather_list(whole, "fsdp", inner, f"agf{color}"))
    pieces = [gathered[color][f] for f in range(inner) for color in range(COLORS)]
    group = PIECE // width
    weights = [
        pieces[k] if group == 1 else jnp.concatenate(pieces[k * group : (k + 1) * group], 1)
        for k in range(COLUMNS // PIECE)
    ]
    w_qk, w_vo, w_up, w_down = weights[0], weights[1], weights[2:4], weights[4:6]
    w_v, w_o = w_vo[:, :MODEL_WIDTH], w_vo[:, MODEL_WIDTH:]

    with jax.named_scope("lookup"):
        looked = take_rows(wanted, embedding).reshape(outer, inner, cap, shard_cols)
        with jax.named_scope("reply"):
            replies = lax.all_to_all(looked, "dp", 0, 0, tiled=True)
    own_part = replies[:, 0].reshape(slots, shard_cols)
    other_parts = [
        swap_by(replies[:, d].reshape(slots, shard_cols), "fsdp", inner, d, "reply_swap") for d in range(1, inner)
    ]
    rows_low = in_order([own_part] + other_parts, inner, 1)
    token_rows = dot((bucket[:, None] == counting[None, :]).astype(BF16), rows_low)

    lengths = seq_lengths.astype(jnp.int32)
    embedded = (token_rows.reshape(seq_count, MAXLEN, MODEL_WIDTH) + positions[None]).reshape(slots, MODEL_WIDTH)
    vectors = norm_vectors[2 : 2 + PER_LAYER]
    bias_q, bias_v, bias_o, bias_d, gain_one, bias_one, gain_two, bias_two = (vectors[k] for k in range(8))
    bias_up = vectors[8:].reshape(2, PIECE)
    hidden, kept_zero = norm_forward(embedded, norm_vectors[0], norm_vectors[1])
    hidden_low = hidden.astype(BF16)
    qk = (dot(hidden_low, w_qk) + jnp.concatenate([bias_q, jnp.zeros_like(bias_q)])).astype(BF16)
    v = (dot(hidden_low, w_v) + bias_v).astype(BF16)
    attended = attend(lengths, qk, v)
    first, kept_one = norm_forward(hidden + (dot(attended, w_o) + bias_o), gain_one, bias_one)
    first_low = first.astype(BF16)
    active, slopes = [], []
    for k in range(2):
        value, slope = gelu_and_slope(dot(first_low, w_up[k]) + bias_up[k])
        active.append(value.astype(BF16))
        slopes.append(slope)
    downward = dot(active[0], w_down[0], CONTRACT_COLS) + dot(active[1], w_down[1], CONTRACT_COLS) + bias_d
    final, kept_two = norm_forward(first + downward, gain_two, bias_two)

    valid = (jnp.arange(MAXLEN)[None, :] < lengths[:, None]).astype(F32)
    lengths_float = lengths.astype(F32)[:, None]
    pooled = jnp.sum(final.reshape(seq_count, MAXLEN, MODEL_WIDTH) * valid[:, :, None], 1) / lengths_float
    with jax.named_scope("pool"):
        all_pooled = everyone(pooled, BOTH, devices).reshape(devices * seq_count, MODEL_WIDTH)
    d_all_pooled, d_projected, loss_out = contrast(all_pooled, head_weight, log_scale)
    loss_value, grad_scale = loss_out[0, 0], loss_out[0, 1]
    device_index = outer_index * inner + inner_index
    d_pooled = lax.dynamic_slice_in_dim(d_all_pooled, device_index * seq_count, seq_count, 0)
    d_final = ((d_pooled / lengths_float)[:, None, :] * valid[:, :, None]).reshape(slots, MODEL_WIDTH)

    def columns_sum(make, whole, name):
        if inner != 2:
            return scatter_bits(whole(), "fsdp", inner, inner_order[::-1], 1, name)
        sent = swap(make(1 - inner_index).astype(BF16), "fsdp", 2, 0, name)
        return make(inner_index) + sent.astype(F32)

    def rows_sum(values, color, name):
        return scatter_bits(values, "dp", outer, scatter_orders[color], 0, name)

    def of_two(half, pair):
        return jnp.where(half == 0, pair[0], pair[1])

    def half_columns(half, values):
        return lax.dynamic_slice_in_dim(values, half * (values.shape[1] // 2), values.shape[1] // 2, 1)

    d_two, d_gain_two, d_bias_two = norm_backward(d_final, kept_two, gain_two)
    d_two_low = d_two.astype(BF16)
    part_down = columns_sum(
        lambda half: dot(d_two_low, of_two(half, active), CONTRACT_ROWS),
        lambda: jnp.concatenate([dot(d_two_low, active[k], CONTRACT_ROWS) for k in range(2)], 1),
        "rsf_down",
    )
    sum_down = rows_sum(part_down, 0, "rs_down")
    d_ups = [slopes[k] * dot(d_two_low, w_down[k]) for k in range(2)]
    d_up_lows = [d_up.astype(BF16) for d_up in d_ups]
    part_up = columns_sum(
        lambda half: dot(first_low, of_two(half, d_up_lows), CONTRACT_ROWS),
        lambda: jnp.concatenate([dot(first_low, d_up_lows[k], CONTRACT_ROWS) for k in range(2)], 1),
        "rsf_up",
    )
    sum_up = rows_sum(part_up, 1, "rs_up")
    d_first = d_two + dot(d_up_lows[0], w_up[0], CONTRACT_COLS) + dot(d_up_lows[1], w_up[1], CONTRACT_COLS)
    d_one, d_gain_one, d_bias_one = norm_backward(d_first, kept_one, gain_one)
    d_one_low = d_one.astype(BF16)
    d_attended = dot(d_one_low, w_o, CONTRACT_COLS).astype(BF16)
    part_out = columns_sum(
        lambda half: dot(attended, half_columns(half, d_one_low), CONTRACT_ROWS),
        lambda: dot(attended, d_one_low, CONTRACT_ROWS),
        "rsf_out",
    )
    sum_out = rows_sum(part_out, 2, "rs_out")
    d_q, d_k, d_v, d_sums = attend_back(lengths, qk, v, d_attended)
    d_hidden = (
        d_one
        + dot(d_q, w_qk[:, :MODEL_WIDTH], CONTRACT_COLS)
        + dot(d_k, w_qk[:, MODEL_WIDTH:], CONTRACT_COLS)
        + dot(d_v, w_v, CONTRACT_COLS)
    )
    d_embedded, d_gain_zero, d_bias_zero = norm_backward(d_hidden, kept_zero, norm_vectors[0])

    d_tokens = d_embedded.astype(BF16)
    back_rows = dot((counting[:, None] == bucket[None, :]).astype(BF16), d_tokens).astype(BF16)
    parts = [
        lax.dynamic_slice_in_dim(back_rows, (inner_index ^ d) * shard_cols, shard_cols, 1) for d in range(inner)
    ]
    parts = parts[:1] + [swap_by(parts[d], "fsdp", inner, d, "back_swap") for d in range(1, inner)]
    back = jnp.concatenate([rows.reshape(outer, 1, cap, shard_cols) for rows in parts], 1)
    with jax.named_scope("back"):
        returned = lax.all_to_all(back, "dp", 0, 0, tiled=True).reshape(entries, shard_cols)

    d_positions = jnp.sum(d_embedded.reshape(seq_count, MAXLEN, MODEL_WIDTH), 0)
    part = MODEL_WIDTH // inner
    part_positions = columns_sum(
        lambda half: half_columns(half, d_positions), lambda: d_positions, "rsf_pos"
    )
    reduced = []
    for color, d_rows in enumerate((d_q, d_k, d_v)):
        block = columns_sum(
            lambda half: dot(hidden_low, half_columns(half, d_rows), CONTRACT_ROWS),
            lambda: dot(hidden_low, d_rows, CONTRACT_ROWS),
            f"rsf_in{color}",
        ).reshape(outer, local_rows, part)
        if color == 0:
            block = jnp.concatenate([block, part_positions.reshape(outer, MAXLEN // outer, part)], 1)
        reduced.append(rows_sum(block, color, f"rs_in{color}")[0])
    own_positions = reduced[0][local_rows:]
    reduced[0] = reduced[0][:local_rows]
    sums = d_sums.reshape(seq_count, 8, MODEL_WIDTH).sum(0)
    d_vectors = jnp.concatenate(
        [
            d_gain_zero,
            d_bias_zero,
            sums[0],
            sums[1],
            jnp.sum(d_one, 0),
            jnp.sum(d_two, 0),
            d_gain_one,
            d_bias_one,
            d_gain_two,
            d_bias_two,
            jnp.sum(d_ups[0], 0),
            jnp.sum(d_ups[1], 0),
        ]
    )
    vector_share = d_vectors.size // devices

    def to_columns(values, name):
        whole = gather_list(values, "fsdp", inner, name)
        return lambda low, high: jnp.concatenate([piece[:, low:high] for piece in whole], 1)

    early = to_columns(jnp.concatenate([sum_out, sum_up, sum_down], 1), "fix_early")
    late = to_columns(jnp.concatenate(reduced, 1), "fix_late")
    cut = [0, part, part + FF // inner, part + 2 * FF // inner]
    full_grad = jnp.concatenate(
        [late(k * part, (k + 1) * part) for k in range(3)] + [early(cut[k], cut[k + 1]) for k in range(3)], 1
    )
    grad_layers = lax.dynamic_slice_in_dim(full_grad, inner_index * local_cols, local_cols, 1)

    entry = jnp.arange(entries, dtype=jnp.int32)
    goes_before = (wanted[None, :] < wanted[:, None]) | (
        (wanted[None, :] == wanted[:, None]) & (entry[None, :] < entry[:, None])
    )
    rank = jnp.sum(goes_before.astype(jnp.int32), 1)
    rows_at = jnp.sum(jnp.where(rank[None, :] == entry[:, None], wanted[None, :], 0), 1)
    is_first = jnp.concatenate([jnp.ones((1,), bool), rows_at[1:] != rows_at[:-1]]).astype(F32)
    tiles = -(-shard_rows // TILE_ROWS)
    starts = jnp.sum(
        (rows_at[None, :] < (jnp.arange(tiles + 1, dtype=jnp.int32) * TILE_ROWS)[:, None]).astype(jnp.int32), 1
    )
    lanes = 128
    high, low_digit = rows_at // lanes, rows_at % lanes
    digits = -(-shard_rows // lanes)
    high_hot = (jnp.arange(digits, dtype=jnp.int32)[:, None] == high[None, :]).astype(F32)
    low_hot = (low_digit[:, None] == jnp.arange(lanes, dtype=jnp.int32)[None, :]).astype(F32)
    own_rows_old = lax.dynamic_slice_in_dim(embed_rows, outer_index * shard_rows, shard_rows)
    dense_old = jnp.pad(own_rows_old, (0, digits * lanes - shard_rows)).reshape(digits, lanes)
    picked = lax.dot_general(high_hot, dense_old, CONTRACT_ROWS, precision=EXACT_PRECISION)
    entry_rows_old = jnp.sum(picked * low_hot, 1)
    embed_square = jnp.sum(embedding * embedding)

    grad_rows = dot((rows_at[:, None] == wanted[None, :]).astype(BF16), returned)
    row_part = jnp.sum(grad_rows * grad_rows, 1)
    row_sums = row_part
    for bit in inner_order:
        row_sums = row_sums + swap(row_sums, "fsdp", inner, bit, "row_swap")
    entry_rows = DECAY_RATE * entry_rows_old + (1.0 - DECAY_RATE) * (row_sums / MODEL_WIDTH + FLOOR_SQUARE)
    scaled_rows = grad_rows * lax.rsqrt(entry_rows)[:, None]
    col_part = jnp.sum(grad_rows * grad_rows * is_first[:, None], 0)
    scaled_part = jnp.sum(scaled_rows * scaled_rows * is_first[:, None], 0)
    common = jnp.concatenate([col_part, scaled_part, jnp.sum(row_part * is_first)[None], embed_square[None]])
    payload = jnp.concatenate(
        [
            jnp.broadcast_to(common[None], (devices, common.size)),
            d_vectors.reshape(devices, vector_share),
        ],
        1,
    )
    payload = jnp.pad(payload, ((0, 0), (0, -payload.shape[1] % 1024))).reshape(devices, -1, 128)
    with jax.named_scope("embed_stats"):
        stats = lax.all_to_all(payload, BOTH, 0, 0, tiled=True).reshape(devices, -1)
    own_vectors = jnp.sum(stats[:, common.size : common.size + vector_share], 0)
    stats = stats[:, : common.size].reshape(outer, inner, common.size).sum(0)
    embed_col_sum = stats[:, :shard_cols].reshape(-1)
    scaled_sum = stats[:, shard_cols : 2 * shard_cols].reshape(-1)
    embed_total, embed_squares = jnp.sum(stats[:, -2]), jnp.sum(stats[:, -1])
    embed_cols_new = DECAY_RATE * embed_cols + (1.0 - DECAY_RATE) * (embed_col_sum / VOCAB + FLOOR_SQUARE)
    rows_mean = DECAY_RATE * jnp.mean(embed_rows) + (1.0 - DECAY_RATE) * (
        embed_total / MODEL_WIDTH / VOCAB + FLOOR_SQUARE
    )
    count = float(VOCAB * MODEL_WIDTH)
    embed_spread = jnp.sqrt(jnp.sum(scaled_sum * (rows_mean / embed_cols_new)) / count)
    embed_step = RELATIVE * jnp.maximum(FLOOR_SCALE, jnp.sqrt(embed_squares / count))
    embed_scale = embed_step / jnp.maximum(1.0, embed_spread / CLIP_LIMIT)
    own_cols = lax.dynamic_slice_in_dim(embed_cols_new, inner_index * shard_cols, shard_cols)
    col_scale = embed_scale * lax.rsqrt(own_cols / rows_mean)
    embedding_new, embedding_copy = table_update(rows_at, starts, embedding, scaled_rows, col_scale[None])
    dense_rows = jnp.dot(
        high_hot, low_hot * (row_sums * is_first)[:, None], precision=EXACT_PRECISION
    ).reshape(-1)

    unit = math.gcd(local_cols, MODEL_WIDTH)
    groups = local_cols // unit
    total_groups = COLUMNS // unit
    bounds = [0, 1, 2, 3, 4, 4 + FF // MODEL_WIDTH, 4 + 2 * FF // MODEL_WIDTH]
    bounds = [b * (MODEL_WIDTH // unit) for b in bounds]
    widths = jnp.array([MODEL_WIDTH] * 4 + [FF] * 2, F32)

    def by_block(values):
        return jnp.stack([jnp.sum(values[..., bounds[b] : bounds[b + 1]], -1) for b in range(6)], -1)

    def by_group(values):
        return jnp.stack([jnp.sum(values[..., g * unit : (g + 1) * unit], -1) for g in range(groups)], -1)

    def own_groups(block_values):
        per_group = jnp.stack([block_values[..., b] for b in range(6) for _ in range(bounds[b + 1] - bounds[b])], -1)
        return lax.dynamic_slice_in_dim(per_group, inner_index * groups, groups, per_group.ndim - 1)

    def over_columns(group_values, columns):
        return jnp.concatenate(
            [jnp.broadcast_to(group_values[:, g : g + 1], (group_values.shape[0], unit)) for g in range(columns)], 1
        )

    layer_square = grad_layers * grad_layers
    row_groups = by_group(layer_square)
    all_groups = jnp.concatenate(gather_list(row_groups, "fsdp", inner, "layer_row_swap"), 1)
    own_row_sums = by_block(all_groups)
    own_rows_before = lax.dynamic_slice_in_dim(layer_rows[0], outer_index * local_rows, local_rows, 1)
    own_layer_rows = DECAY_RATE * own_rows_before.T + (1.0 - DECAY_RATE) * (
        own_row_sums / widths[None, :] + FLOOR_SQUARE
    )
    scaled_grad = grad_layers * over_columns(lax.rsqrt(own_groups(own_layer_rows)), groups)
    weight_groups = jnp.sum(by_group(layers[0] * layers[0]), 0)
    lead = 1024
    payload = jnp.concatenate(
        [
            padded(jnp.concatenate([own_row_sums.reshape(-1), weight_groups]), lead),
            jnp.sum(layer_square, 0),
            jnp.sum(scaled_grad * scaled_grad, 0),
        ]
    )
    with jax.named_scope("layer_stats"):
        stats = everyone(payload.reshape(-1, 128), "dp", outer).reshape(outer, -1)
    row_stats = stats[:, : local_rows * 6].reshape(MODEL_WIDTH, 6)
    layer_rows_new = DECAY_RATE * layer_rows[0] + (1.0 - DECAY_RATE) * (
        row_stats.T / widths[:, None] + FLOOR_SQUARE
    )
    col_stats = jnp.sum(stats[:, local_rows * 6 :], 0)
    own_weight_groups, col_stats = col_stats[:groups], col_stats[lead - local_rows * 6 :]
    own_cols_before = lax.dynamic_slice_in_dim(layer_cols[0], inner_index * local_cols, local_cols, 0)
    own_layer_cols = DECAY_RATE * own_cols_before + (1.0 - DECAY_RATE) * (
        col_stats[:local_cols] / MODEL_WIDTH + FLOOR_SQUARE
    )
    rows_means = jnp.mean(layer_rows_new, -1)
    ratio = col_stats[local_cols:] / own_layer_cols
    own_share = jnp.stack([jnp.sum(ratio[g * unit : (g + 1) * unit]) for g in range(groups)])
    shares = gather_list(
        padded(jnp.concatenate([own_layer_cols, own_share, own_weight_groups]), 1024), "fsdp", inner, "layer_col_swap"
    )
    layer_cols_new = jnp.concatenate([values[:local_cols] for values in shares])
    update_groups = jnp.concatenate([values[local_cols : local_cols + groups] for values in shares])
    weight_groups = jnp.concatenate([values[local_cols + groups : local_cols + 2 * groups] for values in shares])
    counts = MODEL_WIDTH * widths
    spreads = jnp.sqrt(by_block(update_groups) * rows_means / counts)
    layer_scale = (
        RELATIVE
        * jnp.maximum(FLOOR_SCALE, jnp.sqrt(by_block(weight_groups) / counts))
        / jnp.maximum(1.0, spreads / CLIP_LIMIT)
    )
    group_scale = over_columns(own_groups(layer_scale * jnp.sqrt(rows_means))[None], groups)
    layers_new = layers[0] - scaled_grad * (group_scale * lax.rsqrt(own_layer_cols)[None])

    own_dense = dense_rows[:shard_rows]
    share = -(-shard_rows // inner)
    dense_pad = jnp.pad(own_dense, (0, share * inner - shard_rows))
    own_share = lax.dynamic_slice_in_dim(dense_pad, inner_index * share, share)
    flat_part = padded(jnp.concatenate([own_vectors, own_share]), 8 * part).reshape(-1, part)
    pos_rows_count = own_positions.shape[0]
    with jax.named_scope("spread"):
        spread = everyone(jnp.concatenate([own_positions, flat_part], 0), "dp", outer)
    spread = gather_list(spread, "fsdp", inner, "spread_swap")
    grad_pos = jnp.concatenate([values[:, :pos_rows_count].reshape(MAXLEN, part) for values in spread], 1)
    flats = [values[:, pos_rows_count:].reshape(outer, -1) for values in spread]
    grad_vectors = jnp.stack([values[:, :vector_share] for values in flats], 1).reshape(norm_vectors.shape)
    embed_row_sum = jnp.concatenate([values[:, vector_share : vector_share + share] for values in flats], 1)
    embed_row_sum = embed_row_sum[:, :shard_rows].reshape(-1)
    embed_rows_new = DECAY_RATE * embed_rows + (1.0 - DECAY_RATE) * (embed_row_sum / MODEL_WIDTH + FLOOR_SQUARE)

    grad_head = lax.dot_general(all_pooled, d_projected, CONTRACT_ROWS, precision=EXACT_PRECISION)
    head_update, head_rows_new, head_cols_new = factored_step(grad_head, head_rows, head_cols)
    head_new, head_spread = apply_update(head_weight, head_update)
    pos_update, pos_rows_new, pos_cols_new = factored_step(grad_pos, pos_rows, pos_cols)
    positions_new, pos_spread = apply_update(positions, pos_update)
    vector_update, vector_moment_new = plain_step(grad_vectors, vector_moment)
    vectors_new, vector_spread = apply_update(norm_vectors, vector_update)
    scale_update, scale_moment_new = plain_step(grad_scale, scale_moment)
    log_scale_new, scale_spread = apply_update(log_scale, scale_update)
    update_rms = jnp.concatenate(
        [jnp.stack([embed_spread, head_spread, pos_spread, vector_spread, scale_spread]), spreads]
    )
    return (
        loss_value,
        embedding_new,
        embed_rows_new,
        embed_cols_new,
        embedding_copy,
        layers_new[None],
        layer_rows_new[None],
        layer_cols_new[None],
        layers_new.astype(BF16)[None],
        head_new,
        head_rows_new,
        head_cols_new,
        positions_new,
        pos_rows_new,
        pos_cols_new,
        vectors_new,
        vector_moment_new,
        log_scale_new,
        scale_moment_new,
        update_rms,
    )


def solution(mesh):
    split = P("dp", "fsdp")
    layer_split = P(None, "dp", "fsdp")
    whole = P()
    return jax.shard_map(
        body,
        mesh=mesh,
        in_specs=(P(BOTH, None), P(BOTH), split, whole, whole, layer_split) + (whole,) * 12,
        out_specs=(whole, split, whole, whole, split, layer_split, whole, whole, layer_split) + (whole,) * 11,
        check_vma=False,
    )
```

```python
import functools
import math

import jax
import jax.numpy as jnp
from jax import lax
from jax.experimental import pallas as pl
from jax.experimental.pallas import tpu as pltpu
from jax.sharding import PartitionSpec as P


MODEL_WIDTH = 768
HEAD = 64
FF = 3072
VOCAB = 250112
MAXLEN = 512
PER_LAYER = 8 + FF // MODEL_WIDTH
COLUMNS = 4 * MODEL_WIDTH + 2 * FF
PIECE = FF // 2
COLORS = 3
TILE_ROWS = 2048

NORM_EPSILON = 1e-05
UNIT_EPSILON = 1e-06
DECAY_RATE = 0.5
FLOOR_SQUARE = 1e-30
FLOOR_SCALE = 0.001
CLIP_LIMIT = 1.0
RELATIVE = 0.3
EXACT_PRECISION = lax.Precision.HIGHEST
BOTH = ("dp", "fsdp")
F32, BF16 = jnp.float32, jnp.bfloat16
CONTRACT_ROWS = (((0,), (0,)), ((), ()))
CONTRACT_COLS = (((1,), (1,)), ((), ()))
CONTRACT_IN = (((1,), (0,)), ((), ()))


def dot(left, right, dims=CONTRACT_IN):
    return lax.dot_general(left, right, dims, preferred_element_type=F32)


def bit_count(size):
    return size.bit_length() - 1


def bit_orders(size):
    count = bit_count(size)
    rest = list(range(count - 1))[::-1]
    turns = [rest[-k:] + rest[:-k] if k else rest for k in range(COLORS)]
    return [[count - 1] + turn for turn in turns]


def sum_orders(size):
    count = bit_count(size)
    top, rest = [count - 1], list(range(count - 1))
    return [rest[:1] + rest[1:][::-1] + top, rest[1:2] + rest[:1] + rest[2:] + top, rest[::-1] + top]


def swap_by(values, axis, size, mask):
    return lax.ppermute(values, axis, [(i, i ^ mask) for i in range(size)])


def swap(values, axis, size, bit):
    return swap_by(values, axis, size, 1 << bit)


def own_bit(axis, bit):
    return (lax.axis_index(axis) >> bit) & 1


def gather_bits(values, axis, size, order):
    count = bit_count(size)
    held = values.reshape((1,) * count + values.shape)
    for bit in order:
        other = swap(held, axis, size, bit)
        dim = count - 1 - bit
        low_first = jnp.concatenate([held, other], dim)
        high_first = jnp.concatenate([other, held], dim)
        held = jnp.where(own_bit(axis, bit) == 0, low_first, high_first)
    return held.reshape((size,) + values.shape)


def in_order(held, size, dim):
    me = lax.axis_index("fsdp")
    for bit in range(bit_count(size)):
        mine = (me >> bit) & 1
        held = [jnp.where(mine == 0, held[k], held[k ^ (1 << bit)]) for k in range(size)]
    return jnp.concatenate(held, dim)


def gather_list(values, axis, size):
    held = [values] + [swap_by(values, axis, size, d) for d in range(1, size)]
    for bit in range(bit_count(size)):
        mine = own_bit(axis, bit)
        held = [jnp.where(mine == 0, held[k], held[k ^ (1 << bit)]) for k in range(size)]
    return held


def fsdp_others(values, size):
    return [swap_by(values, "fsdp", size, d) for d in range(1, size)]


def scatter_bits(values, axis, size, order, dim):
    for place, bit in enumerate(order):
        shape = values.shape
        half = shape[dim] // 2
        above = 1 << sum(1 for b in order[place + 1 :] if b > bit)
        parts = values.reshape(shape[:dim] + (above, 2, half // above) + shape[dim + 1 :])
        mine = own_bit(axis, bit)
        keep = lax.dynamic_index_in_dim(parts, mine, dim + 1, keepdims=False)
        send = lax.dynamic_index_in_dim(parts, 1 - mine, dim + 1, keepdims=False).astype(BF16)
        rest = shape[:dim] + (half,) + shape[dim + 1 :]
        values = keep.reshape(rest) + swap(send.reshape(rest), axis, size, bit).astype(F32)
    return values


def everyone(values, axis, size):
    return lax.all_to_all(
        jnp.broadcast_to(values[None], (size,) + values.shape), axis, 0, 0, tiled=True
    )


def padded(values, multiple):
    return jnp.pad(values, (0, -values.size % multiple))


def attention_scores(query, key_rows, length):
    scores = dot(query, key_rows, CONTRACT_COLS) * 0.125
    valid = lax.broadcasted_iota(jnp.int32, scores.shape, 1) < length
    scores = jnp.where(valid, scores, -1e30)
    raised = jnp.exp(scores - jnp.max(scores, -1, keepdims=True))
    return raised / jnp.sum(raised, -1, keepdims=True)


def attention_kernel(lengths, q_ref, k_ref, v_ref, o_ref):
    length = lengths[pl.program_id(0)]
    lanes = lax.broadcasted_iota(jnp.int32, q_ref.shape, 1)
    query, key_rows, value_rows = q_ref[...], k_ref[...], v_ref[...]
    zero = jnp.zeros_like(query)
    first = attention_scores(jnp.where(lanes < HEAD, query, zero), key_rows, length)
    second = attention_scores(jnp.where(lanes < HEAD, zero, query), key_rows, length)
    out = jnp.where(lanes < HEAD, dot(first.astype(BF16), value_rows), dot(second.astype(BF16), value_rows))
    o_ref[...] = out.astype(BF16)


def attend(lengths, qk, v):
    seqs = lengths.shape[0]
    pairs = MODEL_WIDTH // 128
    block = (MAXLEN, 128)
    return pl.pallas_call(
        attention_kernel,
        grid_spec=pltpu.PrefetchScalarGridSpec(
            num_scalar_prefetch=1,
            grid=(seqs, pairs),
            in_specs=[
                pl.BlockSpec(block, lambda s, h, n: (s, h)),
                pl.BlockSpec(block, lambda s, h, n: (s, h + pairs)),
                pl.BlockSpec(block, lambda s, h, n: (s, h)),
            ],
            out_specs=pl.BlockSpec(block, lambda s, h, n: (s, h)),
        ),
        out_shape=jax.ShapeDtypeStruct((seqs * MAXLEN, MODEL_WIDTH), BF16),
        name="attend",
    )(lengths, qk, qk, v)


def attention_back_kernel(seq, lengths, q_ref, k_ref, v_ref, d_ref, *refs):
    dq_ref, dk_ref, dv_ref, sum_ref = refs[-4:]
    length = lengths[seq]
    lanes = lax.broadcasted_iota(jnp.int32, q_ref.shape, 1)
    query, key_rows, value_rows, d_rows = q_ref[...], k_ref[...], v_ref[...], d_ref[...]
    zero = jnp.zeros_like(query)
    parts = []
    for low_half in (True, False):
        take = (lanes < HEAD) if low_half else (lanes >= HEAD)
        soft = attention_scores(jnp.where(take, query, zero), key_rows, length)
        d_values = dot(soft.astype(BF16), d_rows, CONTRACT_ROWS)
        d_soft = dot(jnp.where(take, d_rows, zero), value_rows, CONTRACT_COLS)
        d_scores = soft * (d_soft - jnp.sum(soft * d_soft, -1, keepdims=True))
        d_low = d_scores.astype(BF16)
        parts.append((dot(d_low, key_rows) * 0.125, dot(d_low, query, CONTRACT_ROWS) * 0.125, d_values))
    dq, dk, dv = (jnp.where(lanes < HEAD, a, b) for a, b in zip(*parts))
    dq_ref[...] = dq.astype(BF16)
    dk_ref[...] = dk.astype(BF16)
    dv_ref[...] = dv.astype(BF16)
    sums = jnp.concatenate([jnp.sum(dq, 0, keepdims=True), jnp.sum(dv, 0, keepdims=True)], 0)
    sum_ref[...] = jnp.concatenate([sums, jnp.zeros((6, 128), F32)], 0)


def attend_back(seq, lengths, qk, v, d_att, before):
    seqs = lengths.shape[0]
    pairs = MODEL_WIDTH // 128
    block = (MAXLEN, 128)
    plain = pl.BlockSpec(block, lambda h, n: (seq, h))
    low = jax.ShapeDtypeStruct((seqs * MAXLEN, MODEL_WIDTH), BF16)
    return pl.pallas_call(
        functools.partial(attention_back_kernel, seq),
        grid_spec=pltpu.PrefetchScalarGridSpec(
            num_scalar_prefetch=1,
            grid=(pairs,),
            in_specs=[plain, pl.BlockSpec(block, lambda h, n: (seq, h + pairs)), plain, plain]
            + [pl.BlockSpec(memory_space=pl.ANY)] * len(before),
            out_specs=[plain, plain, plain, pl.BlockSpec((8, 128), lambda h, n: (seq, h))],
        ),
        out_shape=[low, low, low, jax.ShapeDtypeStruct((seqs * 8, MODEL_WIDTH), F32)],
        input_output_aliases={5 + k: k for k in range(len(before))},
    )(lengths, qk, qk, v, d_att, *before)


def rows_kernel(wanted, table_ref, out_ref, rows, sem):
    count = rows.shape[0]

    def fetch(j, carry):
        pltpu.make_async_copy(table_ref.at[pl.ds(wanted[j], 1)], rows.at[pl.ds(j, 1)], sem).start()
        return carry

    lax.fori_loop(0, count, fetch, 0, unroll=8)
    pltpu.make_async_copy(rows, rows, sem).wait()
    out_ref[...] = rows[...].astype(BF16)


def take_rows(wanted, table):
    count, width = wanted.shape[0], table.shape[1]
    return pl.pallas_call(
        rows_kernel,
        grid_spec=pltpu.PrefetchScalarGridSpec(
            num_scalar_prefetch=1,
            grid=(1,),
            in_specs=[pl.BlockSpec(memory_space=pl.ANY)],
            out_specs=pl.BlockSpec((count, width), lambda i, n: (0, 0)),
            scratch_shapes=[pltpu.VMEM((count, width), F32), pltpu.SemaphoreType.DMA],
        ),
        out_shape=jax.ShapeDtypeStruct((count, width), BF16),
        name="take_rows",
    )(wanted, table)


def table_kernel(rows_at, starts, table_ref, update_ref, scale_ref, new_ref, low_ref):
    tile = pl.program_id(0)
    base = tile * TILE_ROWS
    scale = scale_ref[...]
    new_ref[...] = table_ref[...]

    def patch(k, carry):
        row = pl.ds(rows_at[k] - base, 1)
        new_ref[row, :] = table_ref[row, :] - scale * update_ref[pl.ds(k, 1), :]
        return carry

    lax.fori_loop(starts[tile], starts[tile + 1], patch, 0)
    low_ref[...] = new_ref[...].astype(BF16)


def table_update(rows_at, starts, table, update, scale):
    height, width = table.shape
    tile = pl.BlockSpec((TILE_ROWS, width), lambda i, *_: (i, 0))
    return pl.pallas_call(
        table_kernel,
        grid_spec=pltpu.PrefetchScalarGridSpec(
            num_scalar_prefetch=2,
            grid=(pl.cdiv(height, TILE_ROWS),),
            in_specs=[
                tile,
                pl.BlockSpec(update.shape, lambda i, *_: (0, 0)),
                pl.BlockSpec(scale.shape, lambda i, *_: (0, 0)),
            ],
            out_specs=[tile, tile],
        ),
        out_shape=[
            jax.ShapeDtypeStruct((height, width), F32),
            jax.ShapeDtypeStruct((height, width), BF16),
        ],
        name="table_update",
    )(rows_at, starts, table, update, scale)


def norm_forward(values, gain_row, bias_row):
    center = values - jnp.mean(values, -1, keepdims=True)
    spread = jnp.mean(center * center, -1, keepdims=True)
    inverse = lax.rsqrt(spread + NORM_EPSILON)
    unit = center * inverse
    return unit * gain_row + bias_row, (unit, inverse)


def norm_backward(d_out, kept, gain_row):
    unit, inverse = kept
    scaled = d_out * gain_row
    d_in = inverse * (
        scaled - jnp.mean(scaled, -1, keepdims=True) - unit * jnp.mean(scaled * unit, -1, keepdims=True)
    )
    return d_in, jnp.sum(d_out * unit, 0), jnp.sum(d_out, 0)


def gelu_and_slope(values):
    normal = 0.5 + 0.5 * lax.erf(values * math.sqrt(0.5))
    slope = normal + values * (jnp.exp(-0.5 * values * values) * (1.0 / math.sqrt(2.0 * math.pi)))
    return values * normal, slope


def exact(left, right, dims=CONTRACT_IN):
    return lax.dot_general(left, right, dims, precision=EXACT_PRECISION, preferred_element_type=F32)


def contrast_kernel(scale_ref, pooled_ref, head_ref, d_pooled_ref, d_projected_ref, loss_ref):
    projected = exact(pooled_ref[...], head_ref[...])
    inverse = lax.rsqrt(jnp.sum(projected * projected, -1, keepdims=True) + UNIT_EPSILON)
    units = projected * inverse
    scale = jnp.exp(jnp.full((1, 1), scale_ref[0], F32))
    logits = scale * exact(units, units, CONTRACT_COLS)
    row = lax.broadcasted_iota(jnp.int32, logits.shape, 0)
    col = lax.broadcasted_iota(jnp.int32, logits.shape, 1)
    used = (row % 2 == 0) & (col % 2 == 1)
    pairs = used & (col == row + 1)
    total = jnp.zeros((1, 1), F32)
    d_logits = jnp.where(pairs, -1.0, 0.0)
    for axis in (1, 0):
        seen = jnp.where(used, logits, -1e30)
        peak = jnp.max(seen, axis, keepdims=True)
        raised = jnp.where(used, jnp.exp(seen - peak), 0.0)
        sums = jnp.sum(raised, axis, keepdims=True)
        safe = jnp.where(sums > 0.0, sums, 1.0)
        d_logits += 0.5 * raised / safe
        logs = jnp.where(sums > 0.0, peak + jnp.log(safe), 0.0)
        total += 0.5 * jnp.sum(jnp.sum(logs, 1, keepdims=True), 0, keepdims=True)
    matched = jnp.where(pairs, logits, 0.0)
    total -= jnp.sum(jnp.sum(matched, 1, keepdims=True), 0, keepdims=True)
    weighted = jnp.where(used, d_logits * logits, 0.0)
    d_scale = jnp.sum(jnp.sum(weighted, 1, keepdims=True), 0, keepdims=True)
    d_units = scale * (exact(d_logits, units) + exact(d_logits, units, CONTRACT_ROWS))
    along = jnp.sum(projected * d_units, -1, keepdims=True)
    d_projected = inverse * d_units - projected * (inverse * inverse * inverse * along)
    d_projected_ref[...] = d_projected
    d_pooled_ref[...] = exact(d_projected, head_ref[...], CONTRACT_COLS)
    lane = lax.broadcasted_iota(jnp.int32, (8, 128), 1)
    loss_ref[...] = jnp.where(lane == 0, total, jnp.where(lane == 1, d_scale, 0.0))


def contrast(pooled, head_weight, log_scale):
    vmem = pl.BlockSpec(memory_space=pltpu.VMEM)
    like = jax.ShapeDtypeStruct(pooled.shape, F32)
    return pl.pallas_call(
        contrast_kernel,
        in_specs=[pl.BlockSpec(memory_space=pltpu.SMEM), vmem, vmem],
        out_specs=[vmem] * 3,
        out_shape=[like, like, jax.ShapeDtypeStruct((8, 128), F32)],
        name="contrast",
    )(log_scale.reshape(1), pooled, head_weight)


def factored_step(gradient, rows_old, cols_old):
    square = gradient * gradient
    rows_new = DECAY_RATE * rows_old + (1.0 - DECAY_RATE) * (jnp.mean(square, 1) + FLOOR_SQUARE)
    cols_new = DECAY_RATE * cols_old + (1.0 - DECAY_RATE) * (jnp.mean(square, 0) + FLOOR_SQUARE)
    estimate = rows_new[:, None] * cols_new[None, :] / jnp.mean(rows_new)
    return (gradient * lax.rsqrt(estimate), rows_new, cols_new)


def plain_step(gradient, moment_old):
    moment_new = DECAY_RATE * moment_old + (1.0 - DECAY_RATE) * (gradient * gradient + FLOOR_SQUARE)
    return (gradient * lax.rsqrt(moment_new), moment_new)


def apply_update(weight_matrix, update):
    spread = jnp.sqrt(jnp.mean(update * update))
    clip_factor = jnp.maximum(1.0, spread / CLIP_LIMIT)
    step_size = RELATIVE * jnp.maximum(FLOOR_SCALE, jnp.sqrt(jnp.mean(weight_matrix * weight_matrix)))
    return (weight_matrix - step_size * (update / clip_factor), spread)


def body(
    token_ids,
    seq_lengths,
    embedding,
    embed_rows,
    embed_cols,
    layers,
    layer_rows,
    layer_cols,
    head_weight,
    head_rows,
    head_cols,
    positions,
    pos_rows,
    pos_cols,
    norm_vectors,
    vector_moment,
    log_scale,
    scale_moment,
):
    outer = lax.axis_size("dp")
    inner = lax.axis_size("fsdp")
    devices = outer * inner
    outer_index = lax.axis_index("dp")
    inner_index = lax.axis_index("fsdp")
    seq_count = token_ids.shape[0]
    slots = seq_count * MAXLEN
    cap = slots // outer
    shard_rows, shard_cols = embedding.shape
    local_rows, local_cols = layers.shape[1], layers.shape[2]
    gather_orders = bit_orders(outer)
    scatter_orders = [order[::-1] for order in gather_orders]
    block_orders = sum_orders(outer)
    inner_order = list(range(bit_count(inner)))

    flat = token_ids.reshape(slots)
    owners = flat // shard_rows
    offsets = flat - owners * shard_rows
    hot = owners[:, None] == jnp.arange(outer, dtype=jnp.int32)[None, :]
    counting = jnp.arange(slots, dtype=jnp.int32)
    before = dot((counting[:, None] >= counting[None, :]).astype(BF16), hot.astype(BF16))
    rank = jnp.sum(jnp.where(hot, before, 0.0), 1).astype(jnp.int32) - 1
    bucket = owners * cap + rank
    outgoing = jnp.sum(jnp.where(counting[:, None] == bucket[None, :], offsets[None, :], 0), 1)
    asked = lax.all_to_all(outgoing.reshape(outer, cap), "dp", 0, 0, tiled=True)
    wanted = jnp.stack([asked] + fsdp_others(asked, inner), 1).reshape(-1)
    entries = wanted.shape[0]

    wanted, forward_vectors, forward_positions, lengths = lax.optimization_barrier(
        (wanted, norm_vectors, positions, seq_lengths.astype(jnp.int32))
    )

    old_rows_mean = jnp.mean(embed_rows)

    low_layers = layers[0].astype(BF16)
    width = local_cols // COLORS
    gathered = []
    for color in range(COLORS):
        piece = low_layers[:, color * width : (color + 1) * width]
        whole = gather_bits(piece, "dp", outer, gather_orders[color]).reshape(MODEL_WIDTH, width)
        gathered.append(gather_list(whole, "fsdp", inner))
    pieces = [gathered[color][f] for f in range(inner) for color in range(COLORS)]
    group = PIECE // width
    weights = [
        pieces[k] if group == 1 else jnp.concatenate(pieces[k * group : (k + 1) * group], 1)
        for k in range(COLUMNS // PIECE)
    ]
    w_qk, w_vo, w_up, w_down = weights[0], weights[1], weights[2:4], weights[4:6]
    w_v, w_o = w_vo[:, :MODEL_WIDTH], w_vo[:, MODEL_WIDTH:]

    looked = take_rows(wanted, embedding).reshape(outer, inner, cap, shard_cols)
    replies = lax.all_to_all(looked, "dp", 0, 0, tiled=True)
    own_part = replies[:, 0].reshape(slots, shard_cols)
    other_parts = [swap_by(replies[:, d].reshape(slots, shard_cols), "fsdp", inner, d) for d in range(1, inner)]
    rows_low = in_order([own_part] + other_parts, inner, 1)
    token_rows = dot((bucket[:, None] == counting[None, :]).astype(BF16), rows_low)

    embedded = (token_rows.reshape(seq_count, MAXLEN, MODEL_WIDTH) + forward_positions[None]).reshape(slots, MODEL_WIDTH)
    vectors = forward_vectors[2 : 2 + PER_LAYER]
    bias_q, bias_v, bias_o, bias_d, gain_one, bias_one, gain_two, bias_two = (vectors[k] for k in range(8))
    bias_up = vectors[8:].reshape(2, PIECE)
    hidden, kept_zero = norm_forward(embedded, forward_vectors[0], forward_vectors[1])
    hidden_low = hidden.astype(BF16)
    qk = (dot(hidden_low, w_qk) + jnp.concatenate([bias_q, jnp.zeros_like(bias_q)])).astype(BF16)
    v = (dot(hidden_low, w_v) + bias_v).astype(BF16)
    attended = attend(lengths, qk, v)
    first, kept_one = norm_forward(hidden + (dot(attended, w_o) + bias_o), gain_one, bias_one)
    first_low = first.astype(BF16)
    active, slopes = [], []
    for k in range(2):
        value, slope = gelu_and_slope(dot(first_low, w_up[k]) + bias_up[k])
        active.append(value.astype(BF16))
        slopes.append(slope)
    downward = dot(active[0], w_down[0], CONTRACT_COLS) + dot(active[1], w_down[1], CONTRACT_COLS) + bias_d
    final, kept_two = norm_forward(first + downward, gain_two, bias_two)

    valid = (jnp.arange(MAXLEN)[None, :] < lengths[:, None]).astype(F32)
    lengths_float = lengths.astype(F32)[:, None]
    pooled = jnp.sum(final.reshape(seq_count, MAXLEN, MODEL_WIDTH) * valid[:, :, None], 1) / lengths_float
    all_pooled = everyone(pooled, BOTH, devices).reshape(devices * seq_count, MODEL_WIDTH)
    d_all_pooled, d_projected, loss_out = contrast(all_pooled, head_weight, log_scale)
    loss_value, grad_scale = loss_out[0, 0], loss_out[0, 1]
    device_index = outer_index * inner + inner_index
    d_pooled = lax.dynamic_slice_in_dim(d_all_pooled, device_index * seq_count, seq_count, 0)
    d_final = ((d_pooled / lengths_float)[:, None, :] * valid[:, :, None]).reshape(slots, MODEL_WIDTH)

    def columns_sum(make, whole):
        if inner != 2:
            return scatter_bits(whole(), "fsdp", inner, inner_order[::-1], 1)
        sent = swap(make(1 - inner_index).astype(BF16), "fsdp", 2, 0)
        return make(inner_index) + sent.astype(F32)

    def rows_sum(values, order):
        return scatter_bits(values, "dp", outer, order, 0)

    def of_two(half, pair):
        return jnp.where(half == 0, pair[0], pair[1])

    def half_columns(half, values):
        return lax.dynamic_slice_in_dim(values, half * (values.shape[1] // 2), values.shape[1] // 2, 1)

    d_two, d_gain_two, d_bias_two = norm_backward(d_final, kept_two, gain_two)
    d_two_low = d_two.astype(BF16)
    part_down = columns_sum(
        lambda half: dot(d_two_low, of_two(half, active), CONTRACT_ROWS),
        lambda: jnp.concatenate([dot(d_two_low, active[k], CONTRACT_ROWS) for k in range(2)], 1),
    )
    sum_down = rows_sum(part_down, block_orders[0])
    d_ups = [slopes[k] * dot(d_two_low, w_down[k]) for k in range(2)]
    d_up_lows = [d_up.astype(BF16) for d_up in d_ups]
    part_up = columns_sum(
        lambda half: dot(first_low, of_two(half, d_up_lows), CONTRACT_ROWS),
        lambda: jnp.concatenate([dot(first_low, d_up_lows[k], CONTRACT_ROWS) for k in range(2)], 1),
    )
    sum_up = rows_sum(part_up, block_orders[1])
    d_first = d_two + dot(d_up_lows[0], w_up[0], CONTRACT_COLS) + dot(d_up_lows[1], w_up[1], CONTRACT_COLS)
    d_one, d_gain_one, d_bias_one = norm_backward(d_first, kept_one, gain_one)
    d_one_low = d_one.astype(BF16)
    d_attended = dot(d_one_low, w_o, CONTRACT_COLS).astype(BF16)
    part_out = columns_sum(
        lambda half: dot(attended, half_columns(half, d_one_low), CONTRACT_ROWS),
        lambda: dot(attended, d_one_low, CONTRACT_ROWS),
    )
    sum_out = rows_sum(part_out, block_orders[2])
    d_heads = ()
    for seq in range(seq_count):
        d_heads = attend_back(seq, lengths, qk, v, d_attended, d_heads)
    d_q, d_k, d_v, d_sums = d_heads
    d_hidden = (
        d_one
        + dot(d_q, w_qk[:, :MODEL_WIDTH], CONTRACT_COLS)
        + dot(d_k, w_qk[:, MODEL_WIDTH:], CONTRACT_COLS)
        + dot(d_v, w_v, CONTRACT_COLS)
    )
    d_embedded, d_gain_zero, d_bias_zero = norm_backward(d_hidden, kept_zero, forward_vectors[0])

    d_tokens = d_embedded.astype(BF16)
    back_rows = dot((counting[:, None] == bucket[None, :]).astype(BF16), d_tokens).astype(BF16)
    parts = [
        lax.dynamic_slice_in_dim(back_rows, (inner_index ^ d) * shard_cols, shard_cols, 1) for d in range(inner)
    ]
    parts = parts[:1] + [swap_by(parts[d], "fsdp", inner, d) for d in range(1, inner)]
    back = jnp.concatenate([rows.reshape(outer, 1, cap, shard_cols) for rows in parts], 1)
    (
        back,
        embed_rows,
        embed_cols,
        layer_rows,
        layer_cols,
        layers,
        head_weight,
        head_rows,
        head_cols,
        positions,
        pos_rows,
        pos_cols,
        norm_vectors,
        vector_moment,
        all_pooled,
        d_projected,
    ) = lax.optimization_barrier(
        (
            back,
            embed_rows,
            embed_cols,
            layer_rows,
            layer_cols,
            layers,
            head_weight,
            head_rows,
            head_cols,
            positions,
            pos_rows,
            pos_cols,
            norm_vectors,
            vector_moment,
            all_pooled,
            d_projected,
        )
    )
    returned = lax.all_to_all(back, "dp", 0, 0, tiled=True).reshape(entries, shard_cols)

    d_positions = jnp.sum(d_embedded.reshape(seq_count, MAXLEN, MODEL_WIDTH), 0)
    part = MODEL_WIDTH // inner
    part_positions = columns_sum(lambda half: half_columns(half, d_positions), lambda: d_positions)
    reduced = []
    for color, d_rows in enumerate((d_q, d_k, d_v)):
        block = columns_sum(
            lambda half: dot(hidden_low, half_columns(half, d_rows), CONTRACT_ROWS),
            lambda: dot(hidden_low, d_rows, CONTRACT_ROWS),
        ).reshape(outer, local_rows, part)
        if color == 0:
            block = jnp.concatenate([block, part_positions.reshape(outer, MAXLEN // outer, part)], 1)
        reduced.append(rows_sum(block, scatter_orders[color])[0])
    own_positions = reduced[0][local_rows:]
    reduced[0] = reduced[0][:local_rows]
    sums = d_sums.reshape(seq_count, 8, MODEL_WIDTH).sum(0)
    d_vectors = jnp.concatenate(
        [
            d_gain_zero,
            d_bias_zero,
            sums[0],
            sums[1],
            jnp.sum(d_one, 0),
            jnp.sum(d_two, 0),
            d_gain_one,
            d_bias_one,
            d_gain_two,
            d_bias_two,
            jnp.sum(d_ups[0], 0),
            jnp.sum(d_ups[1], 0),
        ]
    )
    vector_share = d_vectors.size // devices

    def to_columns(values):
        whole = gather_list(values, "fsdp", inner)
        return lambda low, high: jnp.concatenate([piece[:, low:high] for piece in whole], 1)

    early = to_columns(jnp.concatenate([sum_out, sum_up, sum_down], 1))
    late = to_columns(jnp.concatenate(reduced, 1))
    cut = [0, part, part + FF // inner, part + 2 * FF // inner]
    full_grad = jnp.concatenate(
        [late(k * part, (k + 1) * part) for k in range(3)] + [early(cut[k], cut[k + 1]) for k in range(3)], 1
    )
    grad_layers = lax.dynamic_slice_in_dim(full_grad, inner_index * local_cols, local_cols, 1)

    entry = jnp.arange(entries, dtype=jnp.int32)
    goes_before = (wanted[None, :] < wanted[:, None]) | (
        (wanted[None, :] == wanted[:, None]) & (entry[None, :] < entry[:, None])
    )
    rank = jnp.sum(goes_before.astype(jnp.int32), 1)
    rows_at = jnp.sum(jnp.where(rank[None, :] == entry[:, None], wanted[None, :], 0), 1)
    is_first = jnp.concatenate([jnp.ones((1,), bool), rows_at[1:] != rows_at[:-1]]).astype(F32)
    tiles = -(-shard_rows // TILE_ROWS)
    starts = jnp.sum(
        (rows_at[None, :] < (jnp.arange(tiles + 1, dtype=jnp.int32) * TILE_ROWS)[:, None]).astype(jnp.int32), 1
    )
    lanes = 128
    high, low_digit = rows_at // lanes, rows_at % lanes
    digits = -(-shard_rows // lanes)
    high_hot = (jnp.arange(digits, dtype=jnp.int32)[:, None] == high[None, :]).astype(F32)
    low_hot = (low_digit[:, None] == jnp.arange(lanes, dtype=jnp.int32)[None, :]).astype(F32)
    own_rows_old = lax.dynamic_slice_in_dim(embed_rows, outer_index * shard_rows, shard_rows)
    dense_old = jnp.pad(own_rows_old, (0, digits * lanes - shard_rows)).reshape(digits, lanes)
    picked = lax.dot_general(high_hot, dense_old, CONTRACT_ROWS, precision=EXACT_PRECISION)
    entry_rows_old = jnp.sum(picked * low_hot, 1)
    embed_square = jnp.sum(embedding * embedding)

    grad_rows = dot((rows_at[:, None] == wanted[None, :]).astype(BF16), returned)
    row_part = jnp.sum(grad_rows * grad_rows, 1)
    row_sums = row_part
    for bit in inner_order:
        row_sums = row_sums + swap(row_sums, "fsdp", inner, bit)
    entry_rows = DECAY_RATE * entry_rows_old + (1.0 - DECAY_RATE) * (row_sums / MODEL_WIDTH + FLOOR_SQUARE)
    scaled_rows = grad_rows * lax.rsqrt(entry_rows)[:, None]
    col_part = jnp.sum(grad_rows * grad_rows * is_first[:, None], 0)
    scaled_part = jnp.sum(scaled_rows * scaled_rows * is_first[:, None], 0)
    common = jnp.concatenate([col_part, scaled_part, jnp.sum(row_part * is_first)[None], embed_square[None]])
    payload = jnp.concatenate(
        [
            jnp.broadcast_to(common[None], (devices, common.size)),
            d_vectors.reshape(devices, vector_share),
        ],
        1,
    )
    payload = jnp.pad(payload, ((0, 0), (0, -payload.shape[1] % 1024))).reshape(devices, -1, 128)
    stats = lax.all_to_all(payload, BOTH, 0, 0, tiled=True).reshape(devices, -1)
    own_vectors = jnp.sum(stats[:, common.size : common.size + vector_share], 0)
    embed_stats = own_vectors
    stats = stats[:, : common.size].reshape(outer, inner, common.size).sum(0)
    embed_col_sum = stats[:, :shard_cols].reshape(-1)
    scaled_sum = stats[:, shard_cols : 2 * shard_cols].reshape(-1)
    embed_total, embed_squares = jnp.sum(stats[:, -2]), jnp.sum(stats[:, -1])
    embed_cols_new = DECAY_RATE * embed_cols + (1.0 - DECAY_RATE) * (embed_col_sum / VOCAB + FLOOR_SQUARE)
    rows_mean = DECAY_RATE * old_rows_mean + (1.0 - DECAY_RATE) * (
        embed_total / MODEL_WIDTH / VOCAB + FLOOR_SQUARE
    )
    count = float(VOCAB * MODEL_WIDTH)
    embed_spread = jnp.sqrt(jnp.sum(scaled_sum * (rows_mean / embed_cols_new)) / count)
    embed_step = RELATIVE * jnp.maximum(FLOOR_SCALE, jnp.sqrt(embed_squares / count))
    embed_scale = embed_step / jnp.maximum(1.0, embed_spread / CLIP_LIMIT)
    own_cols = lax.dynamic_slice_in_dim(embed_cols_new, inner_index * shard_cols, shard_cols)
    col_scale = embed_scale * lax.rsqrt(own_cols / rows_mean)
    embedding_new, embedding_copy = table_update(rows_at, starts, embedding, scaled_rows, col_scale[None])
    dense_rows = jnp.dot(
        high_hot, low_hot * (row_sums * is_first)[:, None], precision=EXACT_PRECISION
    ).reshape(-1)

    unit = math.gcd(local_cols, MODEL_WIDTH)
    groups = local_cols // unit
    bounds = [0, 1, 2, 3, 4, 4 + FF // MODEL_WIDTH, 4 + 2 * FF // MODEL_WIDTH]
    bounds = [b * (MODEL_WIDTH // unit) for b in bounds]
    widths = jnp.array([MODEL_WIDTH] * 4 + [FF] * 2, F32)

    def by_block(values):
        return jnp.stack([jnp.sum(values[..., bounds[b] : bounds[b + 1]], -1) for b in range(6)], -1)

    def by_group(values):
        return jnp.stack([jnp.sum(values[..., g * unit : (g + 1) * unit], -1) for g in range(groups)], -1)

    def own_groups(block_values):
        per_group = jnp.stack([block_values[..., b] for b in range(6) for _ in range(bounds[b + 1] - bounds[b])], -1)
        return lax.dynamic_slice_in_dim(per_group, inner_index * groups, groups, per_group.ndim - 1)

    def over_columns(group_values, columns):
        return jnp.concatenate(
            [jnp.broadcast_to(group_values[:, g : g + 1], (group_values.shape[0], unit)) for g in range(columns)], 1
        )

    layer_square = grad_layers * grad_layers
    row_groups = by_group(layer_square)
    all_groups = jnp.concatenate(gather_list(row_groups, "fsdp", inner), 1)
    own_row_sums = by_block(all_groups)
    own_rows_before = lax.dynamic_slice_in_dim(layer_rows[0], outer_index * local_rows, local_rows, 1)
    own_layer_rows = DECAY_RATE * own_rows_before.T + (1.0 - DECAY_RATE) * (
        own_row_sums / widths[None, :] + FLOOR_SQUARE
    )
    scaled_grad = grad_layers * over_columns(lax.rsqrt(own_groups(own_layer_rows)), groups)
    weight_groups = jnp.sum(by_group(layers[0] * layers[0]), 0)
    lead = 1024
    payload = jnp.concatenate(
        [
            padded(jnp.concatenate([own_row_sums.reshape(-1), weight_groups]), lead),
            jnp.sum(layer_square, 0),
            jnp.sum(scaled_grad * scaled_grad, 0),
        ]
    )
    payload, _ = lax.optimization_barrier((payload, embed_stats))
    stats = everyone(payload.reshape(-1, 128), "dp", outer).reshape(outer, -1)
    row_stats = stats[:, : local_rows * 6].reshape(MODEL_WIDTH, 6)
    layer_rows_new = DECAY_RATE * layer_rows[0] + (1.0 - DECAY_RATE) * (
        row_stats.T / widths[:, None] + FLOOR_SQUARE
    )
    col_stats = jnp.sum(stats[:, local_rows * 6 :], 0)
    own_weight_groups, col_stats = col_stats[:groups], col_stats[lead - local_rows * 6 :]
    own_cols_before = lax.dynamic_slice_in_dim(layer_cols[0], inner_index * local_cols, local_cols, 0)
    own_layer_cols = DECAY_RATE * own_cols_before + (1.0 - DECAY_RATE) * (
        col_stats[:local_cols] / MODEL_WIDTH + FLOOR_SQUARE
    )
    rows_means = jnp.mean(layer_rows_new, -1)
    ratio = col_stats[local_cols:] / own_layer_cols
    own_share = jnp.stack([jnp.sum(ratio[g * unit : (g + 1) * unit]) for g in range(groups)])
    shares = gather_list(padded(jnp.concatenate([own_layer_cols, own_share, own_weight_groups]), 1024), "fsdp", inner)
    layer_cols_new = jnp.concatenate([values[:local_cols] for values in shares])
    update_groups = jnp.concatenate([values[local_cols : local_cols + groups] for values in shares])
    weight_groups = jnp.concatenate([values[local_cols + groups : local_cols + 2 * groups] for values in shares])
    counts = MODEL_WIDTH * widths
    spreads = jnp.sqrt(by_block(update_groups) * rows_means / counts)
    layer_scale = (
        RELATIVE
        * jnp.maximum(FLOOR_SCALE, jnp.sqrt(by_block(weight_groups) / counts))
        / jnp.maximum(1.0, spreads / CLIP_LIMIT)
    )
    group_scale = own_groups(layer_scale * jnp.sqrt(rows_means))
    col_factor = (lax.rsqrt(own_layer_cols).reshape(groups, unit) * group_scale[:, None]).reshape(1, local_cols)
    layers_new = layers[0] - scaled_grad * col_factor

    own_dense = dense_rows[:shard_rows]
    share = -(-shard_rows // inner)
    dense_pad = jnp.pad(own_dense, (0, share * inner - shard_rows))
    own_share = lax.dynamic_slice_in_dim(dense_pad, inner_index * share, share)
    flat_part = padded(jnp.concatenate([own_vectors, own_share]), 8 * part).reshape(-1, part)
    pos_rows_count = own_positions.shape[0]
    payload, _ = lax.optimization_barrier((jnp.concatenate([own_positions, flat_part], 0), stats))
    spread = everyone(payload, "dp", outer)
    spread = gather_list(spread, "fsdp", inner)
    grad_pos = jnp.concatenate([values[:, :pos_rows_count].reshape(MAXLEN, part) for values in spread], 1)
    flats = [values[:, pos_rows_count:].reshape(outer, -1) for values in spread]
    grad_vectors = jnp.stack([values[:, :vector_share] for values in flats], 1).reshape(norm_vectors.shape)
    embed_row_sum = jnp.concatenate([values[:, vector_share : vector_share + share] for values in flats], 1)
    embed_row_sum = embed_row_sum[:, :shard_rows].reshape(-1)
    embed_rows_new = DECAY_RATE * embed_rows + (1.0 - DECAY_RATE) * (embed_row_sum / MODEL_WIDTH + FLOOR_SQUARE)

    grad_head = lax.dot_general(all_pooled, d_projected, CONTRACT_ROWS, precision=EXACT_PRECISION)
    head_update, head_rows_new, head_cols_new = factored_step(grad_head, head_rows, head_cols)
    head_new, head_spread = apply_update(head_weight, head_update)
    pos_update, pos_rows_new, pos_cols_new = factored_step(grad_pos, pos_rows, pos_cols)
    positions_new, pos_spread = apply_update(positions, pos_update)
    vector_update, vector_moment_new = plain_step(grad_vectors, vector_moment)
    vectors_new, vector_spread = apply_update(norm_vectors, vector_update)
    scale_update, scale_moment_new = plain_step(grad_scale, scale_moment)
    log_scale_new, scale_spread = apply_update(log_scale, scale_update)
    update_rms = jnp.concatenate(
        [jnp.stack([embed_spread, head_spread, pos_spread, vector_spread, scale_spread]), spreads]
    )
    return (
        loss_value,
        embedding_new,
        embed_rows_new,
        embed_cols_new,
        embedding_copy,
        layers_new[None],
        layer_rows_new[None],
        layer_cols_new[None],
        layers_new.astype(BF16)[None],
        head_new,
        head_rows_new,
        head_cols_new,
        positions_new,
        pos_rows_new,
        pos_cols_new,
        vectors_new,
        vector_moment_new,
        log_scale_new,
        scale_moment_new,
        update_rms,
    )


def solution(mesh):
    split = P("dp", "fsdp")
    layer_split = P(None, "dp", "fsdp")
    whole = P()
    return jax.shard_map(
        body,
        mesh=mesh,
        in_specs=(P(BOTH, None), P(BOTH), split, whole, whole, layer_split) + (whole,) * 12,
        out_specs=(whole, split, whole, whole, split, layer_split, whole, whole, layer_split) + (whole,) * 11,
        check_vma=False,
    )
```

```python
import functools
import math

import jax
import jax.numpy as jnp
from jax import lax
from jax.experimental import pallas as pl
from jax.experimental.pallas import tpu as pltpu
from jax.sharding import PartitionSpec as P


MODEL_WIDTH = 768
HEAD = 64
FF = 3072
VOCAB = 250112
MAXLEN = 512
PER_LAYER = 8 + FF // MODEL_WIDTH
COLUMNS = 4 * MODEL_WIDTH + 2 * FF
PIECE = FF // 2
COLORS = 3
TILE_ROWS = 2048

NORM_EPSILON = 1e-05
UNIT_EPSILON = 1e-06
DECAY_RATE = 0.5
FLOOR_SQUARE = 1e-30
FLOOR_SCALE = 0.001
CLIP_LIMIT = 1.0
RELATIVE = 0.3
EXACT_PRECISION = lax.Precision.HIGHEST
BOTH = ("dp", "fsdp")
F32, BF16 = jnp.float32, jnp.bfloat16
CONTRACT_ROWS = (((0,), (0,)), ((), ()))
CONTRACT_COLS = (((1,), (1,)), ((), ()))
CONTRACT_IN = (((1,), (0,)), ((), ()))


def dot(left, right, dims=CONTRACT_IN):
    return lax.dot_general(left, right, dims, preferred_element_type=F32)


def bit_count(size):
    return size.bit_length() - 1


def bit_orders(size):
    count = bit_count(size)
    rest = list(range(count - 1))[::-1]
    turns = [rest[-k:] + rest[:-k] if k else rest for k in range(COLORS)]
    return [[count - 1] + turn for turn in turns]


def sum_orders(size):
    count = bit_count(size)
    top, rest = [count - 1], list(range(count - 1))
    return [rest[:1] + rest[1:][::-1] + top, rest[1:2] + rest[:1] + rest[2:] + top, rest[::-1] + top]


def swap_by(values, axis, size, mask):
    return lax.ppermute(values, axis, [(i, i ^ mask) for i in range(size)])


def swap(values, axis, size, bit):
    return swap_by(values, axis, size, 1 << bit)


def own_bit(axis, bit):
    return (lax.axis_index(axis) >> bit) & 1


def gather_bits(values, axis, size, order):
    count = bit_count(size)
    held = values.reshape((1,) * count + values.shape)
    for bit in order:
        other = swap(held, axis, size, bit)
        dim = count - 1 - bit
        low_first = jnp.concatenate([held, other], dim)
        high_first = jnp.concatenate([other, held], dim)
        held = jnp.where(own_bit(axis, bit) == 0, low_first, high_first)
    return held.reshape((size,) + values.shape)


def in_order(held, size, dim):
    me = lax.axis_index("fsdp")
    for bit in range(bit_count(size)):
        mine = (me >> bit) & 1
        held = [jnp.where(mine == 0, held[k], held[k ^ (1 << bit)]) for k in range(size)]
    return jnp.concatenate(held, dim)


def gather_list(values, axis, size):
    held = [values] + [swap_by(values, axis, size, d) for d in range(1, size)]
    for bit in range(bit_count(size)):
        mine = own_bit(axis, bit)
        held = [jnp.where(mine == 0, held[k], held[k ^ (1 << bit)]) for k in range(size)]
    return held


def fsdp_others(values, size):
    return [swap_by(values, "fsdp", size, d) for d in range(1, size)]


def scatter_bits(values, axis, size, order, dim):
    for place, bit in enumerate(order):
        shape = values.shape
        half = shape[dim] // 2
        above = 1 << sum(1 for b in order[place + 1 :] if b > bit)
        parts = values.reshape(shape[:dim] + (above, 2, half // above) + shape[dim + 1 :])
        mine = own_bit(axis, bit)
        keep = lax.dynamic_index_in_dim(parts, mine, dim + 1, keepdims=False)
        send = lax.dynamic_index_in_dim(parts, 1 - mine, dim + 1, keepdims=False).astype(BF16)
        rest = shape[:dim] + (half,) + shape[dim + 1 :]
        values = keep.reshape(rest) + swap(send.reshape(rest), axis, size, bit).astype(F32)
    return values


def everyone(values, axis, size):
    return lax.all_to_all(
        jnp.broadcast_to(values[None], (size,) + values.shape), axis, 0, 0, tiled=True
    )


def padded(values, multiple):
    return jnp.pad(values, (0, -values.size % multiple))


def attention_scores(query, key_rows, length):
    scores = dot(query, key_rows, CONTRACT_COLS) * 0.125
    valid = lax.broadcasted_iota(jnp.int32, scores.shape, 1) < length
    scores = jnp.where(valid, scores, -1e30)
    raised = jnp.exp(scores - jnp.max(scores, -1, keepdims=True))
    return raised / jnp.sum(raised, -1, keepdims=True)


def attention_kernel(lengths, q_ref, k_ref, v_ref, o_ref):
    length = lengths[pl.program_id(0)]
    lanes = lax.broadcasted_iota(jnp.int32, q_ref.shape, 1)
    query, key_rows, value_rows = q_ref[...], k_ref[...], v_ref[...]
    zero = jnp.zeros_like(query)
    first = attention_scores(jnp.where(lanes < HEAD, query, zero), key_rows, length)
    second = attention_scores(jnp.where(lanes < HEAD, zero, query), key_rows, length)
    out = jnp.where(lanes < HEAD, dot(first.astype(BF16), value_rows), dot(second.astype(BF16), value_rows))
    o_ref[...] = out.astype(BF16)


def attend(lengths, qk, v):
    seqs = lengths.shape[0]
    pairs = MODEL_WIDTH // 128
    block = (MAXLEN, 128)
    return pl.pallas_call(
        attention_kernel,
        grid_spec=pltpu.PrefetchScalarGridSpec(
            num_scalar_prefetch=1,
            grid=(seqs, pairs),
            in_specs=[
                pl.BlockSpec(block, lambda s, h, n: (s, h)),
                pl.BlockSpec(block, lambda s, h, n: (s, h + pairs)),
                pl.BlockSpec(block, lambda s, h, n: (s, h)),
            ],
            out_specs=pl.BlockSpec(block, lambda s, h, n: (s, h)),
        ),
        out_shape=jax.ShapeDtypeStruct((seqs * MAXLEN, MODEL_WIDTH), BF16),
        name="attend",
    )(lengths, qk, qk, v)


def attention_back_kernel(seq, lengths, q_ref, k_ref, v_ref, d_ref, *refs):
    dq_ref, dk_ref, dv_ref, sum_ref = refs[-4:]
    length = lengths[seq]
    lanes = lax.broadcasted_iota(jnp.int32, q_ref.shape, 1)
    query, key_rows, value_rows, d_rows = q_ref[...], k_ref[...], v_ref[...], d_ref[...]
    zero = jnp.zeros_like(query)
    parts = []
    for low_half in (True, False):
        take = (lanes < HEAD) if low_half else (lanes >= HEAD)
        soft = attention_scores(jnp.where(take, query, zero), key_rows, length)
        d_values = dot(soft.astype(BF16), d_rows, CONTRACT_ROWS)
        d_soft = dot(jnp.where(take, d_rows, zero), value_rows, CONTRACT_COLS)
        d_scores = soft * (d_soft - jnp.sum(soft * d_soft, -1, keepdims=True))
        d_low = d_scores.astype(BF16)
        parts.append((dot(d_low, key_rows) * 0.125, dot(d_low, query, CONTRACT_ROWS) * 0.125, d_values))
    dq, dk, dv = (jnp.where(lanes < HEAD, a, b) for a, b in zip(*parts))
    dq_ref[...] = dq.astype(BF16)
    dk_ref[...] = dk.astype(BF16)
    dv_ref[...] = dv.astype(BF16)
    sums = jnp.concatenate([jnp.sum(dq, 0, keepdims=True), jnp.sum(dv, 0, keepdims=True)], 0)
    sum_ref[...] = jnp.concatenate([sums, jnp.zeros((6, 128), F32)], 0)


def attend_back(seq, lengths, qk, v, d_att, before):
    seqs = lengths.shape[0]
    pairs = MODEL_WIDTH // 128
    block = (MAXLEN, 128)
    plain = pl.BlockSpec(block, lambda h, n: (seq, h))
    low = jax.ShapeDtypeStruct((seqs * MAXLEN, MODEL_WIDTH), BF16)
    return pl.pallas_call(
        functools.partial(attention_back_kernel, seq),
        grid_spec=pltpu.PrefetchScalarGridSpec(
            num_scalar_prefetch=1,
            grid=(pairs,),
            in_specs=[plain, pl.BlockSpec(block, lambda h, n: (seq, h + pairs)), plain, plain]
            + [pl.BlockSpec(memory_space=pl.ANY)] * len(before),
            out_specs=[plain, plain, plain, pl.BlockSpec((8, 128), lambda h, n: (seq, h))],
        ),
        out_shape=[low, low, low, jax.ShapeDtypeStruct((seqs * 8, MODEL_WIDTH), F32)],
        input_output_aliases={5 + k: k for k in range(len(before))},
    )(lengths, qk, qk, v, d_att, *before)


def rows_kernel(wanted, table_ref, out_ref, rows, sem):
    count = rows.shape[0]

    def fetch(j, carry):
        pltpu.make_async_copy(table_ref.at[pl.ds(wanted[j], 1)], rows.at[pl.ds(j, 1)], sem).start()
        return carry

    lax.fori_loop(0, count, fetch, 0, unroll=8)
    pltpu.make_async_copy(rows, rows, sem).wait()
    out_ref[...] = rows[...].astype(BF16)


def take_rows(wanted, table):
    count, width = wanted.shape[0], table.shape[1]
    return pl.pallas_call(
        rows_kernel,
        grid_spec=pltpu.PrefetchScalarGridSpec(
            num_scalar_prefetch=1,
            grid=(1,),
            in_specs=[pl.BlockSpec(memory_space=pl.ANY)],
            out_specs=pl.BlockSpec((count, width), lambda i, n: (0, 0)),
            scratch_shapes=[pltpu.VMEM((count, width), F32), pltpu.SemaphoreType.DMA],
        ),
        out_shape=jax.ShapeDtypeStruct((count, width), BF16),
        name="take_rows",
    )(wanted, table)


def table_kernel(rows_at, starts, table_ref, update_ref, scale_ref, new_ref, low_ref):
    tile = pl.program_id(0)
    base = tile * TILE_ROWS
    scale = scale_ref[...]
    new_ref[...] = table_ref[...]

    def patch(k, carry):
        row = pl.ds(rows_at[k] - base, 1)
        new_ref[row, :] = table_ref[row, :] - scale * update_ref[pl.ds(k, 1), :]
        return carry

    lax.fori_loop(starts[tile], starts[tile + 1], patch, 0)
    low_ref[...] = new_ref[...].astype(BF16)


def table_update(rows_at, starts, table, update, scale):
    height, width = table.shape
    tile = pl.BlockSpec((TILE_ROWS, width), lambda i, *_: (i, 0))
    return pl.pallas_call(
        table_kernel,
        grid_spec=pltpu.PrefetchScalarGridSpec(
            num_scalar_prefetch=2,
            grid=(pl.cdiv(height, TILE_ROWS),),
            in_specs=[
                tile,
                pl.BlockSpec(update.shape, lambda i, *_: (0, 0)),
                pl.BlockSpec(scale.shape, lambda i, *_: (0, 0)),
            ],
            out_specs=[tile, tile],
        ),
        out_shape=[
            jax.ShapeDtypeStruct((height, width), F32),
            jax.ShapeDtypeStruct((height, width), BF16),
        ],
        name="table_update",
    )(rows_at, starts, table, update, scale)


def norm_forward(values, gain_row, bias_row):
    center = values - jnp.mean(values, -1, keepdims=True)
    spread = jnp.mean(center * center, -1, keepdims=True)
    inverse = lax.rsqrt(spread + NORM_EPSILON)
    unit = center * inverse
    return unit * gain_row + bias_row, (unit, inverse)


def norm_backward(d_out, kept, gain_row):
    unit, inverse = kept
    scaled = d_out * gain_row
    d_in = inverse * (
        scaled - jnp.mean(scaled, -1, keepdims=True) - unit * jnp.mean(scaled * unit, -1, keepdims=True)
    )
    return d_in, jnp.sum(d_out * unit, 0), jnp.sum(d_out, 0)


def gelu_and_slope(values):
    normal = 0.5 + 0.5 * lax.erf(values * math.sqrt(0.5))
    slope = normal + values * (jnp.exp(-0.5 * values * values) * (1.0 / math.sqrt(2.0 * math.pi)))
    return values * normal, slope


def exact(left, right, dims=CONTRACT_IN):
    return lax.dot_general(left, right, dims, precision=EXACT_PRECISION, preferred_element_type=F32)


def contrast_kernel(scale_ref, pooled_ref, head_ref, d_pooled_ref, d_projected_ref, loss_ref):
    projected = exact(pooled_ref[...], head_ref[...])
    inverse = lax.rsqrt(jnp.sum(projected * projected, -1, keepdims=True) + UNIT_EPSILON)
    units = projected * inverse
    scale = jnp.exp(jnp.full((1, 1), scale_ref[0], F32))
    logits = scale * exact(units, units, CONTRACT_COLS)
    row = lax.broadcasted_iota(jnp.int32, logits.shape, 0)
    col = lax.broadcasted_iota(jnp.int32, logits.shape, 1)
    used = (row % 2 == 0) & (col % 2 == 1)
    pairs = used & (col == row + 1)
    total = jnp.zeros((1, 1), F32)
    d_logits = jnp.where(pairs, -1.0, 0.0)
    for axis in (1, 0):
        seen = jnp.where(used, logits, -1e30)
        peak = jnp.max(seen, axis, keepdims=True)
        raised = jnp.where(used, jnp.exp(seen - peak), 0.0)
        sums = jnp.sum(raised, axis, keepdims=True)
        safe = jnp.where(sums > 0.0, sums, 1.0)
        d_logits += 0.5 * raised / safe
        logs = jnp.where(sums > 0.0, peak + jnp.log(safe), 0.0)
        total += 0.5 * jnp.sum(jnp.sum(logs, 1, keepdims=True), 0, keepdims=True)
    matched = jnp.where(pairs, logits, 0.0)
    total -= jnp.sum(jnp.sum(matched, 1, keepdims=True), 0, keepdims=True)
    weighted = jnp.where(used, d_logits * logits, 0.0)
    d_scale = jnp.sum(jnp.sum(weighted, 1, keepdims=True), 0, keepdims=True)
    d_units = scale * (exact(d_logits, units) + exact(d_logits, units, CONTRACT_ROWS))
    along = jnp.sum(projected * d_units, -1, keepdims=True)
    d_projected = inverse * d_units - projected * (inverse * inverse * inverse * along)
    d_projected_ref[...] = d_projected
    d_pooled_ref[...] = exact(d_projected, head_ref[...], CONTRACT_COLS)
    lane = lax.broadcasted_iota(jnp.int32, (8, 128), 1)
    loss_ref[...] = jnp.where(lane == 0, total, jnp.where(lane == 1, d_scale, 0.0))


def contrast(pooled, head_weight, log_scale):
    vmem = pl.BlockSpec(memory_space=pltpu.VMEM)
    like = jax.ShapeDtypeStruct(pooled.shape, F32)
    return pl.pallas_call(
        contrast_kernel,
        in_specs=[pl.BlockSpec(memory_space=pltpu.SMEM), vmem, vmem],
        out_specs=[vmem] * 3,
        out_shape=[like, like, jax.ShapeDtypeStruct((8, 128), F32)],
        name="contrast",
    )(log_scale.reshape(1), pooled, head_weight)


def factored_step(gradient, rows_old, cols_old):
    square = gradient * gradient
    rows_new = DECAY_RATE * rows_old + (1.0 - DECAY_RATE) * (jnp.mean(square, 1) + FLOOR_SQUARE)
    cols_new = DECAY_RATE * cols_old + (1.0 - DECAY_RATE) * (jnp.mean(square, 0) + FLOOR_SQUARE)
    estimate = rows_new[:, None] * cols_new[None, :] / jnp.mean(rows_new)
    return (gradient * lax.rsqrt(estimate), rows_new, cols_new)


def plain_step(gradient, moment_old):
    moment_new = DECAY_RATE * moment_old + (1.0 - DECAY_RATE) * (gradient * gradient + FLOOR_SQUARE)
    return (gradient * lax.rsqrt(moment_new), moment_new)


def apply_update(weight_matrix, update, square):
    spread = jnp.sqrt(jnp.mean(update * update))
    clip_factor = jnp.maximum(1.0, spread / CLIP_LIMIT)
    step_size = RELATIVE * jnp.maximum(FLOOR_SCALE, jnp.sqrt(square))
    return (weight_matrix - step_size * (update / clip_factor), spread)


def body(
    token_ids,
    seq_lengths,
    embedding,
    embed_rows,
    embed_cols,
    layers,
    layer_rows,
    layer_cols,
    head_weight,
    head_rows,
    head_cols,
    positions,
    pos_rows,
    pos_cols,
    norm_vectors,
    vector_moment,
    log_scale,
    scale_moment,
):
    outer = lax.axis_size("dp")
    inner = lax.axis_size("fsdp")
    devices = outer * inner
    outer_index = lax.axis_index("dp")
    inner_index = lax.axis_index("fsdp")
    seq_count = token_ids.shape[0]
    slots = seq_count * MAXLEN
    cap = slots // outer
    shard_rows, shard_cols = embedding.shape
    local_rows, local_cols = layers.shape[1], layers.shape[2]
    gather_orders = bit_orders(outer)
    scatter_orders = [order[::-1] for order in gather_orders]
    block_orders = sum_orders(outer)
    inner_order = list(range(bit_count(inner)))

    flat = token_ids.reshape(slots)
    owners = flat // shard_rows
    offsets = flat - owners * shard_rows
    hot = owners[:, None] == jnp.arange(outer, dtype=jnp.int32)[None, :]
    counting = jnp.arange(slots, dtype=jnp.int32)
    before = dot((counting[:, None] >= counting[None, :]).astype(BF16), hot.astype(BF16))
    rank = jnp.sum(jnp.where(hot, before, 0.0), 1).astype(jnp.int32) - 1
    bucket = owners * cap + rank
    outgoing = jnp.sum(jnp.where(counting[:, None] == bucket[None, :], offsets[None, :], 0), 1)
    asked = lax.all_to_all(outgoing.reshape(outer, cap), "dp", 0, 0, tiled=True)
    wanted = jnp.stack([asked] + fsdp_others(asked, inner), 1).reshape(-1)
    entries = wanted.shape[0]

    wanted, forward_vectors, forward_positions, lengths = lax.optimization_barrier(
        (wanted, norm_vectors, positions, seq_lengths.astype(jnp.int32))
    )

    old_rows_mean = jnp.mean(embed_rows)

    low_layers = layers[0].astype(BF16)
    width = local_cols // COLORS
    gathered = []
    for color in range(COLORS):
        piece = low_layers[:, color * width : (color + 1) * width]
        whole = gather_bits(piece, "dp", outer, gather_orders[color]).reshape(MODEL_WIDTH, width)
        gathered.append(gather_list(whole, "fsdp", inner))
    pieces = [gathered[color][f] for f in range(inner) for color in range(COLORS)]
    group = PIECE // width
    weights = [
        pieces[k] if group == 1 else jnp.concatenate(pieces[k * group : (k + 1) * group], 1)
        for k in range(COLUMNS // PIECE)
    ]
    w_qk, w_vo, w_up, w_down = weights[0], weights[1], weights[2:4], weights[4:6]
    w_v, w_o = w_vo[:, :MODEL_WIDTH], w_vo[:, MODEL_WIDTH:]

    looked = take_rows(wanted, embedding).reshape(outer, inner, cap, shard_cols)
    looked, *early = lax.optimization_barrier((looked, head_weight, positions, norm_vectors, layers[0]))
    replies = lax.all_to_all(looked, "dp", 0, 0, tiled=True)
    head_square, pos_square, vector_square = (jnp.mean(weight * weight) for weight in early[:3])
    layer_column_squares = jnp.sum(early[3] * early[3], 0)
    own_part = replies[:, 0].reshape(slots, shard_cols)
    other_parts = [swap_by(replies[:, d].reshape(slots, shard_cols), "fsdp", inner, d) for d in range(1, inner)]
    rows_low = in_order([own_part] + other_parts, inner, 1)
    token_rows = dot((bucket[:, None] == counting[None, :]).astype(BF16), rows_low)

    embedded = (token_rows.reshape(seq_count, MAXLEN, MODEL_WIDTH) + forward_positions[None]).reshape(slots, MODEL_WIDTH)
    vectors = forward_vectors[2 : 2 + PER_LAYER]
    bias_q, bias_v, bias_o, bias_d, gain_one, bias_one, gain_two, bias_two = (vectors[k] for k in range(8))
    bias_up = vectors[8:].reshape(2, PIECE)
    hidden, kept_zero = norm_forward(embedded, forward_vectors[0], forward_vectors[1])
    hidden_low = hidden.astype(BF16)
    qk = (dot(hidden_low, w_qk) + jnp.concatenate([bias_q, jnp.zeros_like(bias_q)])).astype(BF16)
    v = (dot(hidden_low, w_v) + bias_v).astype(BF16)
    attended = attend(lengths, qk, v)
    first, kept_one = norm_forward(hidden + (dot(attended, w_o) + bias_o), gain_one, bias_one)
    first_low = first.astype(BF16)
    active, slopes = [], []
    for k in range(2):
        value, slope = gelu_and_slope(dot(first_low, w_up[k]) + bias_up[k])
        active.append(value.astype(BF16))
        slopes.append(slope)
    downward = dot(active[0], w_down[0], CONTRACT_COLS) + dot(active[1], w_down[1], CONTRACT_COLS) + bias_d
    final, kept_two = norm_forward(first + downward, gain_two, bias_two)

    valid = (jnp.arange(MAXLEN)[None, :] < lengths[:, None]).astype(F32)
    lengths_float = lengths.astype(F32)[:, None]
    pooled = jnp.sum(final.reshape(seq_count, MAXLEN, MODEL_WIDTH) * valid[:, :, None], 1) / lengths_float
    all_pooled = everyone(pooled, BOTH, devices).reshape(devices * seq_count, MODEL_WIDTH)
    d_all_pooled, d_projected, loss_out = contrast(all_pooled, head_weight, log_scale)
    loss_value, grad_scale = loss_out[0, 0], loss_out[0, 1]
    device_index = outer_index * inner + inner_index
    d_pooled = lax.dynamic_slice_in_dim(d_all_pooled, device_index * seq_count, seq_count, 0)
    d_final = ((d_pooled / lengths_float)[:, None, :] * valid[:, :, None]).reshape(slots, MODEL_WIDTH)

    def columns_sum(make, whole):
        if inner != 2:
            return scatter_bits(whole(), "fsdp", inner, inner_order[::-1], 1)
        sent = swap(make(1 - inner_index).astype(BF16), "fsdp", 2, 0)
        return make(inner_index) + sent.astype(F32)

    def rows_sum(values, order):
        return scatter_bits(values, "dp", outer, order, 0)

    def of_two(half, pair):
        return jnp.where(half == 0, pair[0], pair[1])

    def half_columns(half, values):
        return lax.dynamic_slice_in_dim(values, half * (values.shape[1] // 2), values.shape[1] // 2, 1)

    d_two, d_gain_two, d_bias_two = norm_backward(d_final, kept_two, gain_two)
    d_two_low = d_two.astype(BF16)
    part_down = columns_sum(
        lambda half: dot(d_two_low, of_two(half, active), CONTRACT_ROWS),
        lambda: jnp.concatenate([dot(d_two_low, active[k], CONTRACT_ROWS) for k in range(2)], 1),
    )
    sum_down = rows_sum(part_down, block_orders[0])
    d_ups = [slopes[k] * dot(d_two_low, w_down[k]) for k in range(2)]
    d_up_lows = [d_up.astype(BF16) for d_up in d_ups]
    part_up = columns_sum(
        lambda half: dot(first_low, of_two(half, d_up_lows), CONTRACT_ROWS),
        lambda: jnp.concatenate([dot(first_low, d_up_lows[k], CONTRACT_ROWS) for k in range(2)], 1),
    )
    sum_up = rows_sum(part_up, block_orders[1])
    d_first = d_two + dot(d_up_lows[0], w_up[0], CONTRACT_COLS) + dot(d_up_lows[1], w_up[1], CONTRACT_COLS)
    d_one, d_gain_one, d_bias_one = norm_backward(d_first, kept_one, gain_one)
    d_one_low = d_one.astype(BF16)
    d_attended = dot(d_one_low, w_o, CONTRACT_COLS).astype(BF16)
    part_out = columns_sum(
        lambda half: dot(attended, half_columns(half, d_one_low), CONTRACT_ROWS),
        lambda: dot(attended, d_one_low, CONTRACT_ROWS),
    )
    sum_out = rows_sum(part_out, block_orders[2])
    d_heads = ()
    for seq in range(seq_count):
        d_heads = attend_back(seq, lengths, qk, v, d_attended, d_heads)
    d_q, d_k, d_v, d_sums = d_heads
    d_hidden = (
        d_one
        + dot(d_q, w_qk[:, :MODEL_WIDTH], CONTRACT_COLS)
        + dot(d_k, w_qk[:, MODEL_WIDTH:], CONTRACT_COLS)
        + dot(d_v, w_v, CONTRACT_COLS)
    )
    d_embedded, d_gain_zero, d_bias_zero = norm_backward(d_hidden, kept_zero, forward_vectors[0])

    d_tokens = d_embedded.astype(BF16)
    back_rows = dot((counting[:, None] == bucket[None, :]).astype(BF16), d_tokens).astype(BF16)
    parts = [
        lax.dynamic_slice_in_dim(back_rows, (inner_index ^ d) * shard_cols, shard_cols, 1) for d in range(inner)
    ]
    parts = parts[:1] + [swap_by(parts[d], "fsdp", inner, d) for d in range(1, inner)]
    back = jnp.concatenate([rows.reshape(outer, 1, cap, shard_cols) for rows in parts], 1)
    (
        back,
        d_embedded,
        d_q,
        d_k,
        d_v,
        embed_rows,
        embed_cols,
        layer_rows,
        layer_cols,
        layers,
        head_weight,
        head_rows,
        head_cols,
        positions,
        pos_rows,
        pos_cols,
        norm_vectors,
        vector_moment,
        all_pooled,
        d_projected,
    ) = lax.optimization_barrier(
        (
            back,
            d_embedded,
            d_q,
            d_k,
            d_v,
            embed_rows,
            embed_cols,
            layer_rows,
            layer_cols,
            layers,
            head_weight,
            head_rows,
            head_cols,
            positions,
            pos_rows,
            pos_cols,
            norm_vectors,
            vector_moment,
            all_pooled,
            d_projected,
        )
    )
    returned = lax.all_to_all(back, "dp", 0, 0, tiled=True).reshape(entries, shard_cols)

    head_sums = d_sums.reshape(seq_count, 8, MODEL_WIDTH).sum(0)
    d_bias_out, d_bias_down = jnp.sum(d_one, 0), jnp.sum(d_two, 0)
    d_bias_ups = [jnp.sum(d_up, 0) for d_up in d_ups]
    d_positions = jnp.sum(d_embedded.reshape(seq_count, MAXLEN, MODEL_WIDTH), 0)
    part = MODEL_WIDTH // inner
    part_positions = columns_sum(lambda half: half_columns(half, d_positions), lambda: d_positions)
    reduced = []
    for color, d_rows in enumerate((d_q, d_k, d_v)):
        block = columns_sum(
            lambda half: dot(hidden_low, half_columns(half, d_rows), CONTRACT_ROWS),
            lambda: dot(hidden_low, d_rows, CONTRACT_ROWS),
        ).reshape(outer, local_rows, part)
        if color == 0:
            block = jnp.concatenate([block, part_positions.reshape(outer, MAXLEN // outer, part)], 1)
        reduced.append(rows_sum(block, scatter_orders[color])[0])
    own_positions = reduced[0][local_rows:]
    reduced[0] = reduced[0][:local_rows]
    vector_rows = [
        d_gain_zero,
        d_bias_zero,
        head_sums[0],
        head_sums[1],
        d_bias_out,
        d_bias_down,
        d_gain_one,
        d_bias_one,
        d_gain_two,
        d_bias_two,
    ]
    for sums in d_bias_ups:
        vector_rows += [sums[k * MODEL_WIDTH : (k + 1) * MODEL_WIDTH] for k in range(PIECE // MODEL_WIDTH)]
    row_index = jnp.arange(len(vector_rows))[:, None]
    d_vectors = jnp.zeros((len(vector_rows), MODEL_WIDTH), F32)
    for k, row in enumerate(vector_rows):
        d_vectors = jnp.where(row_index == k, row[None, :], d_vectors)
    vector_share = d_vectors.size // devices

    def to_columns(values):
        whole = gather_list(values, "fsdp", inner)
        return lambda low, high: jnp.concatenate([piece[:, low:high] for piece in whole], 1)

    early = to_columns(jnp.concatenate([sum_out, sum_up, sum_down], 1))
    late = to_columns(jnp.concatenate(reduced, 1))
    cut = [0, part, part + FF // inner, part + 2 * FF // inner]
    full_grad = jnp.concatenate(
        [late(k * part, (k + 1) * part) for k in range(3)] + [early(cut[k], cut[k + 1]) for k in range(3)], 1
    )
    grad_layers = lax.dynamic_slice_in_dim(full_grad, inner_index * local_cols, local_cols, 1)

    entry = jnp.arange(entries, dtype=jnp.int32)
    goes_before = (wanted[None, :] < wanted[:, None]) | (
        (wanted[None, :] == wanted[:, None]) & (entry[None, :] < entry[:, None])
    )
    rank = jnp.sum(goes_before.astype(jnp.int32), 1)
    rows_at = jnp.sum(jnp.where(rank[None, :] == entry[:, None], wanted[None, :], 0), 1)
    is_first = jnp.concatenate([jnp.ones((1,), bool), rows_at[1:] != rows_at[:-1]]).astype(F32)
    tiles = -(-shard_rows // TILE_ROWS)
    starts = jnp.sum(
        (rows_at[None, :] < (jnp.arange(tiles + 1, dtype=jnp.int32) * TILE_ROWS)[:, None]).astype(jnp.int32), 1
    )
    lanes = 128
    high, low_digit = rows_at // lanes, rows_at % lanes
    digits = -(-shard_rows // lanes)
    high_hot = (jnp.arange(digits, dtype=jnp.int32)[:, None] == high[None, :]).astype(F32)
    low_hot = (low_digit[:, None] == jnp.arange(lanes, dtype=jnp.int32)[None, :]).astype(F32)
    own_rows_old = lax.dynamic_slice_in_dim(embed_rows, outer_index * shard_rows, shard_rows)
    dense_old = jnp.pad(own_rows_old, (0, digits * lanes - shard_rows)).reshape(digits, lanes)
    picked = lax.dot_general(high_hot, dense_old, CONTRACT_ROWS, precision=EXACT_PRECISION)
    entry_rows_old = jnp.sum(picked * low_hot, 1)
    embed_square = jnp.sum(embedding * embedding)

    grad_rows = dot((rows_at[:, None] == wanted[None, :]).astype(BF16), returned)
    row_part = jnp.sum(grad_rows * grad_rows, 1)
    row_sums = row_part
    for bit in inner_order:
        row_sums = row_sums + swap(row_sums, "fsdp", inner, bit)
    entry_rows = DECAY_RATE * entry_rows_old + (1.0 - DECAY_RATE) * (row_sums / MODEL_WIDTH + FLOOR_SQUARE)
    scaled_rows = grad_rows * lax.rsqrt(entry_rows)[:, None]
    col_part = jnp.sum(grad_rows * grad_rows * is_first[:, None], 0)
    scaled_part = jnp.sum(scaled_rows * scaled_rows * is_first[:, None], 0)
    common = jnp.concatenate([col_part, scaled_part, jnp.sum(row_part * is_first)[None], embed_square[None]])
    payload = jnp.concatenate(
        [
            jnp.broadcast_to(common[None], (devices, common.size)),
            d_vectors.reshape(devices, vector_share),
        ],
        1,
    )
    payload = jnp.pad(payload, ((0, 0), (0, -payload.shape[1] % 1024))).reshape(devices, -1, 128)
    stats = lax.all_to_all(payload, BOTH, 0, 0, tiled=True).reshape(devices, -1)
    own_vectors = jnp.sum(stats[:, common.size : common.size + vector_share], 0)
    embed_stats = own_vectors
    stats = stats[:, : common.size].reshape(outer, inner, common.size).sum(0)
    embed_col_sum = stats[:, :shard_cols].reshape(-1)
    scaled_sum = stats[:, shard_cols : 2 * shard_cols].reshape(-1)
    embed_total, embed_squares = jnp.sum(stats[:, -2]), jnp.sum(stats[:, -1])
    embed_cols_new = DECAY_RATE * embed_cols + (1.0 - DECAY_RATE) * (embed_col_sum / VOCAB + FLOOR_SQUARE)
    rows_mean = DECAY_RATE * old_rows_mean + (1.0 - DECAY_RATE) * (
        embed_total / MODEL_WIDTH / VOCAB + FLOOR_SQUARE
    )
    count = float(VOCAB * MODEL_WIDTH)
    embed_spread = jnp.sqrt(jnp.sum(scaled_sum * (rows_mean / embed_cols_new)) / count)
    embed_step = RELATIVE * jnp.maximum(FLOOR_SCALE, jnp.sqrt(embed_squares / count))
    embed_scale = embed_step / jnp.maximum(1.0, embed_spread / CLIP_LIMIT)
    own_cols = lax.dynamic_slice_in_dim(embed_cols_new, inner_index * shard_cols, shard_cols)
    col_scale = embed_scale * lax.rsqrt(own_cols / rows_mean)
    embedding_new, embedding_copy = table_update(rows_at, starts, embedding, scaled_rows, col_scale[None])
    dense_rows = jnp.dot(
        high_hot, low_hot * (row_sums * is_first)[:, None], precision=EXACT_PRECISION
    ).reshape(-1)

    unit = math.gcd(local_cols, MODEL_WIDTH)
    groups = local_cols // unit
    bounds = [0, 1, 2, 3, 4, 4 + FF // MODEL_WIDTH, 4 + 2 * FF // MODEL_WIDTH]
    bounds = [b * (MODEL_WIDTH // unit) for b in bounds]
    widths = jnp.array([MODEL_WIDTH] * 4 + [FF] * 2, F32)

    def by_block(values):
        return jnp.stack([jnp.sum(values[..., bounds[b] : bounds[b + 1]], -1) for b in range(6)], -1)

    def by_group(values):
        return jnp.stack([jnp.sum(values[..., g * unit : (g + 1) * unit], -1) for g in range(groups)], -1)

    def own_groups(block_values):
        per_group = jnp.stack([block_values[..., b] for b in range(6) for _ in range(bounds[b + 1] - bounds[b])], -1)
        return lax.dynamic_slice_in_dim(per_group, inner_index * groups, groups, per_group.ndim - 1)

    def over_columns(group_values, columns):
        return jnp.concatenate(
            [jnp.broadcast_to(group_values[:, g : g + 1], (group_values.shape[0], unit)) for g in range(columns)], 1
        )

    layer_square = grad_layers * grad_layers
    row_groups = by_group(layer_square)
    all_groups = jnp.concatenate(gather_list(row_groups, "fsdp", inner), 1)
    own_row_sums = by_block(all_groups)
    own_rows_before = lax.dynamic_slice_in_dim(layer_rows[0], outer_index * local_rows, local_rows, 1)
    own_layer_rows = DECAY_RATE * own_rows_before.T + (1.0 - DECAY_RATE) * (
        own_row_sums / widths[None, :] + FLOOR_SQUARE
    )
    scaled_grad = grad_layers * over_columns(lax.rsqrt(own_groups(own_layer_rows)), groups)
    weight_groups = by_group(layer_column_squares)
    lead = 1024
    payload = jnp.concatenate(
        [
            padded(jnp.concatenate([own_row_sums.reshape(-1), weight_groups]), lead),
            jnp.sum(layer_square, 0),
            jnp.sum(scaled_grad * scaled_grad, 0),
        ]
    )
    payload = jnp.concatenate([payload.reshape(-1, 128), padded(own_positions.reshape(-1), 1024).reshape(-1, 128)], 0)
    payload, _ = lax.optimization_barrier((payload, embed_stats))
    stats_rows = (lead + 2 * local_cols) // 128
    stats = everyone(payload, "dp", outer)
    stats, pos_stats = stats[:, :stats_rows].reshape(outer, -1), stats[:, stats_rows:].reshape(outer, -1)
    pos_stats = pos_stats[:, : own_positions.size].reshape(MAXLEN, part)
    grad_pos = jnp.concatenate(gather_list(pos_stats, "fsdp", inner), 1)
    row_stats = stats[:, : local_rows * 6].reshape(MODEL_WIDTH, 6)
    layer_rows_new = DECAY_RATE * layer_rows[0] + (1.0 - DECAY_RATE) * (
        row_stats.T / widths[:, None] + FLOOR_SQUARE
    )
    col_stats = jnp.sum(stats[:, local_rows * 6 :], 0)
    own_weight_groups, col_stats = col_stats[:groups], col_stats[lead - local_rows * 6 :]
    own_cols_before = lax.dynamic_slice_in_dim(layer_cols[0], inner_index * local_cols, local_cols, 0)
    own_layer_cols = DECAY_RATE * own_cols_before + (1.0 - DECAY_RATE) * (
        col_stats[:local_cols] / MODEL_WIDTH + FLOOR_SQUARE
    )
    rows_means = jnp.mean(layer_rows_new, -1)
    ratio = col_stats[local_cols:] / own_layer_cols
    own_share = jnp.stack([jnp.sum(ratio[g * unit : (g + 1) * unit]) for g in range(groups)])
    shares = gather_list(padded(jnp.concatenate([own_layer_cols, own_share, own_weight_groups]), 1024), "fsdp", inner)
    layer_cols_new = jnp.concatenate([values[:local_cols] for values in shares])
    update_groups = jnp.concatenate([values[local_cols : local_cols + groups] for values in shares])
    weight_groups = jnp.concatenate([values[local_cols + groups : local_cols + 2 * groups] for values in shares])
    counts = MODEL_WIDTH * widths
    spreads = jnp.sqrt(by_block(update_groups) * rows_means / counts)
    layer_scale = (
        RELATIVE
        * jnp.maximum(FLOOR_SCALE, jnp.sqrt(by_block(weight_groups) / counts))
        / jnp.maximum(1.0, spreads / CLIP_LIMIT)
    )
    group_scale = own_groups(layer_scale * jnp.sqrt(rows_means))
    col_factor = (lax.rsqrt(own_layer_cols).reshape(groups, unit) * group_scale[:, None]).reshape(1, local_cols)
    layers_new = layers[0] - scaled_grad * col_factor

    own_dense = dense_rows[:shard_rows]
    share = -(-shard_rows // inner)
    dense_pad = jnp.pad(own_dense, (0, share * inner - shard_rows))
    own_share = lax.dynamic_slice_in_dim(dense_pad, inner_index * share, share)
    flat_part = padded(jnp.concatenate([own_vectors, own_share]), 1024).reshape(-1, 128)
    payload, _ = lax.optimization_barrier((flat_part, stats))
    spread = everyone(payload, "dp", outer)
    spread = gather_list(spread, "fsdp", inner)
    flats = [values.reshape(outer, -1) for values in spread]
    grad_vectors = jnp.stack([values[:, :vector_share] for values in flats], 1).reshape(norm_vectors.shape)
    embed_row_sum = jnp.concatenate([values[:, vector_share : vector_share + share] for values in flats], 1)
    embed_row_sum = embed_row_sum[:, :shard_rows].reshape(-1)
    embed_rows_new = DECAY_RATE * embed_rows + (1.0 - DECAY_RATE) * (embed_row_sum / MODEL_WIDTH + FLOOR_SQUARE)

    grad_head = lax.dot_general(all_pooled, d_projected, CONTRACT_ROWS, precision=EXACT_PRECISION)
    head_update, head_rows_new, head_cols_new = factored_step(grad_head, head_rows, head_cols)
    head_new, head_spread = apply_update(head_weight, head_update, head_square)
    pos_update, pos_rows_new, pos_cols_new = factored_step(grad_pos, pos_rows, pos_cols)
    positions_new, pos_spread = apply_update(positions, pos_update, pos_square)
    vector_update, vector_moment_new = plain_step(grad_vectors, vector_moment)
    vectors_new, vector_spread = apply_update(norm_vectors, vector_update, vector_square)
    scale_update, scale_moment_new = plain_step(grad_scale, scale_moment)
    log_scale_new, scale_spread = apply_update(log_scale, scale_update, log_scale * log_scale)
    update_rms = jnp.concatenate(
        [jnp.stack([embed_spread, head_spread, pos_spread, vector_spread, scale_spread]), spreads]
    )
    return (
        loss_value,
        embedding_new,
        embed_rows_new,
        embed_cols_new,
        embedding_copy,
        layers_new[None],
        layer_rows_new[None],
        layer_cols_new[None],
        layers_new.astype(BF16)[None],
        head_new,
        head_rows_new,
        head_cols_new,
        positions_new,
        pos_rows_new,
        pos_cols_new,
        vectors_new,
        vector_moment_new,
        log_scale_new,
        scale_moment_new,
        update_rms,
    )


def solution(mesh):
    split = P("dp", "fsdp")
    layer_split = P(None, "dp", "fsdp")
    whole = P()
    return jax.shard_map(
        body,
        mesh=mesh,
        in_specs=(P(BOTH, None), P(BOTH), split, whole, whole, layer_split) + (whole,) * 12,
        out_specs=(whole, split, whole, whole, split, layer_split, whole, whole, layer_split) + (whole,) * 11,
        check_vma=False,
    )
```

```python
import functools
import math

import jax
import jax.numpy as jnp
from jax import lax
from jax.experimental import pallas as pl
from jax.experimental.pallas import tpu as pltpu
from jax.sharding import PartitionSpec as P


MODEL_WIDTH = 768
HEAD = 64
FF = 3072
VOCAB = 250112
MAXLEN = 512
PER_LAYER = 8 + FF // MODEL_WIDTH
COLUMNS = 4 * MODEL_WIDTH + 2 * FF
PIECE = FF // 2
COLORS = 3
TILE_ROWS = 2048

NORM_EPSILON = 1e-05
UNIT_EPSILON = 1e-06
DECAY_RATE = 0.5
FLOOR_SQUARE = 1e-30
FLOOR_SCALE = 0.001
CLIP_LIMIT = 1.0
RELATIVE = 0.3
EXACT_PRECISION = lax.Precision.HIGHEST
BOTH = ("dp", "fsdp")
F32, BF16 = jnp.float32, jnp.bfloat16
CONTRACT_ROWS = (((0,), (0,)), ((), ()))
CONTRACT_COLS = (((1,), (1,)), ((), ()))
CONTRACT_IN = (((1,), (0,)), ((), ()))


def dot(left, right, dims=CONTRACT_IN):
    return lax.dot_general(left, right, dims, preferred_element_type=F32)


def bit_count(size):
    return size.bit_length() - 1


def bit_orders(size):
    count = bit_count(size)
    rest = list(range(count - 1))[::-1]
    turns = [rest[-k:] + rest[:-k] if k else rest for k in range(COLORS)]
    return [[count - 1] + turn for turn in turns]


def sum_orders(size):
    count = bit_count(size)
    top, rest = [count - 1], list(range(count - 1))
    return [rest[:1] + rest[1:][::-1] + top, rest[1:2] + rest[:1] + rest[2:] + top, rest[::-1] + top]


def swap_by(values, axis, size, mask):
    return lax.ppermute(values, axis, [(i, i ^ mask) for i in range(size)])


def swap(values, axis, size, bit):
    return swap_by(values, axis, size, 1 << bit)


def own_bit(axis, bit):
    return (lax.axis_index(axis) >> bit) & 1


def gather_bits(values, axis, size, order):
    count = bit_count(size)
    held = values.reshape((1,) * count + values.shape)
    for bit in order:
        other = swap(held, axis, size, bit)
        dim = count - 1 - bit
        low_first = jnp.concatenate([held, other], dim)
        high_first = jnp.concatenate([other, held], dim)
        held = jnp.where(own_bit(axis, bit) == 0, low_first, high_first)
    return held.reshape((size,) + values.shape)


def in_order(held, size, dim):
    me = lax.axis_index("fsdp")
    for bit in range(bit_count(size)):
        mine = (me >> bit) & 1
        held = [jnp.where(mine == 0, held[k], held[k ^ (1 << bit)]) for k in range(size)]
    return jnp.concatenate(held, dim)


def gather_list(values, axis, size):
    held = [values] + [swap_by(values, axis, size, d) for d in range(1, size)]
    for bit in range(bit_count(size)):
        mine = own_bit(axis, bit)
        held = [jnp.where(mine == 0, held[k], held[k ^ (1 << bit)]) for k in range(size)]
    return held


def fsdp_others(values, size):
    return [swap_by(values, "fsdp", size, d) for d in range(1, size)]


def scatter_bits(values, axis, size, order, dim):
    for place, bit in enumerate(order):
        shape = values.shape
        half = shape[dim] // 2
        above = 1 << sum(1 for b in order[place + 1 :] if b > bit)
        parts = values.reshape(shape[:dim] + (above, 2, half // above) + shape[dim + 1 :])
        mine = own_bit(axis, bit)
        keep = lax.dynamic_index_in_dim(parts, mine, dim + 1, keepdims=False)
        send = lax.dynamic_index_in_dim(parts, 1 - mine, dim + 1, keepdims=False).astype(BF16)
        rest = shape[:dim] + (half,) + shape[dim + 1 :]
        values = keep.reshape(rest) + swap(send.reshape(rest), axis, size, bit).astype(F32)
    return values


def everyone(values, axis, size):
    return lax.all_to_all(
        jnp.broadcast_to(values[None], (size,) + values.shape), axis, 0, 0, tiled=True
    )


def padded(values, multiple):
    return jnp.pad(values, (0, -values.size % multiple))


def attention_scores(query, key_rows, length):
    scores = dot(query, key_rows, CONTRACT_COLS) * 0.125
    valid = lax.broadcasted_iota(jnp.int32, scores.shape, 1) < length
    scores = jnp.where(valid, scores, -1e30)
    raised = jnp.exp(scores - jnp.max(scores, -1, keepdims=True))
    return raised / jnp.sum(raised, -1, keepdims=True)


def attention_kernel(lengths, q_ref, k_ref, v_ref, o_ref):
    length = lengths[pl.program_id(0)]
    lanes = lax.broadcasted_iota(jnp.int32, q_ref.shape, 1)
    query, key_rows, value_rows = q_ref[...], k_ref[...], v_ref[...]
    zero = jnp.zeros_like(query)
    first = attention_scores(jnp.where(lanes < HEAD, query, zero), key_rows, length)
    second = attention_scores(jnp.where(lanes < HEAD, zero, query), key_rows, length)
    out = jnp.where(lanes < HEAD, dot(first.astype(BF16), value_rows), dot(second.astype(BF16), value_rows))
    o_ref[...] = out.astype(BF16)


def attend(lengths, qk, v):
    seqs = lengths.shape[0]
    pairs = MODEL_WIDTH // 128
    block = (MAXLEN, 128)
    return pl.pallas_call(
        attention_kernel,
        grid_spec=pltpu.PrefetchScalarGridSpec(
            num_scalar_prefetch=1,
            grid=(seqs, pairs),
            in_specs=[
                pl.BlockSpec(block, lambda s, h, n: (s, h)),
                pl.BlockSpec(block, lambda s, h, n: (s, h + pairs)),
                pl.BlockSpec(block, lambda s, h, n: (s, h)),
            ],
            out_specs=pl.BlockSpec(block, lambda s, h, n: (s, h)),
        ),
        out_shape=jax.ShapeDtypeStruct((seqs * MAXLEN, MODEL_WIDTH), BF16),
        name="attend",
    )(lengths, qk, qk, v)


def attention_back_kernel(seq, lengths, q_ref, k_ref, v_ref, d_ref, *refs):
    dq_ref, dk_ref, dv_ref, sum_ref = refs[-4:]
    length = lengths[seq]
    lanes = lax.broadcasted_iota(jnp.int32, q_ref.shape, 1)
    query, key_rows, value_rows, d_rows = q_ref[...], k_ref[...], v_ref[...], d_ref[...]
    zero = jnp.zeros_like(query)
    parts = []
    for low_half in (True, False):
        take = (lanes < HEAD) if low_half else (lanes >= HEAD)
        soft = attention_scores(jnp.where(take, query, zero), key_rows, length)
        d_values = dot(soft.astype(BF16), d_rows, CONTRACT_ROWS)
        d_soft = dot(jnp.where(take, d_rows, zero), value_rows, CONTRACT_COLS)
        d_scores = soft * (d_soft - jnp.sum(soft * d_soft, -1, keepdims=True))
        d_low = d_scores.astype(BF16)
        parts.append((dot(d_low, key_rows) * 0.125, dot(d_low, query, CONTRACT_ROWS) * 0.125, d_values))
    dq, dk, dv = (jnp.where(lanes < HEAD, a, b) for a, b in zip(*parts))
    dq_ref[...] = dq.astype(BF16)
    dk_ref[...] = dk.astype(BF16)
    dv_ref[...] = dv.astype(BF16)
    sums = jnp.concatenate([jnp.sum(dq, 0, keepdims=True), jnp.sum(dv, 0, keepdims=True)], 0)
    sum_ref[...] = jnp.concatenate([sums, jnp.zeros((6, 128), F32)], 0)


def attend_back(seq, lengths, qk, v, d_att, before):
    seqs = lengths.shape[0]
    pairs = MODEL_WIDTH // 128
    block = (MAXLEN, 128)
    plain = pl.BlockSpec(block, lambda h, n: (seq, h))
    low = jax.ShapeDtypeStruct((seqs * MAXLEN, MODEL_WIDTH), BF16)
    return pl.pallas_call(
        functools.partial(attention_back_kernel, seq),
        grid_spec=pltpu.PrefetchScalarGridSpec(
            num_scalar_prefetch=1,
            grid=(pairs,),
            in_specs=[plain, pl.BlockSpec(block, lambda h, n: (seq, h + pairs)), plain, plain]
            + [pl.BlockSpec(memory_space=pl.ANY)] * len(before),
            out_specs=[plain, plain, plain, pl.BlockSpec((8, 128), lambda h, n: (seq, h))],
        ),
        out_shape=[low, low, low, jax.ShapeDtypeStruct((seqs * 8, MODEL_WIDTH), F32)],
        input_output_aliases={5 + k: k for k in range(len(before))},
    )(lengths, qk, qk, v, d_att, *before)


def rows_kernel(wanted, table_ref, out_ref, rows, sem):
    count = rows.shape[0]

    def fetch(j, carry):
        pltpu.make_async_copy(table_ref.at[pl.ds(wanted[j], 1)], rows.at[pl.ds(j, 1)], sem).start()
        return carry

    lax.fori_loop(0, count, fetch, 0, unroll=8)
    pltpu.make_async_copy(rows, rows, sem).wait()
    out_ref[...] = rows[...].astype(BF16)


def take_rows(wanted, table):
    count, width = wanted.shape[0], table.shape[1]
    return pl.pallas_call(
        rows_kernel,
        grid_spec=pltpu.PrefetchScalarGridSpec(
            num_scalar_prefetch=1,
            grid=(1,),
            in_specs=[pl.BlockSpec(memory_space=pl.ANY)],
            out_specs=pl.BlockSpec((count, width), lambda i, n: (0, 0)),
            scratch_shapes=[pltpu.VMEM((count, width), F32), pltpu.SemaphoreType.DMA],
        ),
        out_shape=jax.ShapeDtypeStruct((count, width), BF16),
        name="take_rows",
    )(wanted, table)


def table_kernel(rows_at, starts, table_ref, update_ref, scale_ref, new_ref, low_ref):
    tile = pl.program_id(0)
    base = tile * TILE_ROWS
    scale = scale_ref[...]
    new_ref[...] = table_ref[...]

    def patch(k, carry):
        row = pl.ds(rows_at[k] - base, 1)
        new_ref[row, :] = table_ref[row, :] - scale * update_ref[pl.ds(k, 1), :]
        return carry

    lax.fori_loop(starts[tile], starts[tile + 1], patch, 0)
    low_ref[...] = new_ref[...].astype(BF16)


def table_update(rows_at, starts, table, update, scale):
    height, width = table.shape
    tile = pl.BlockSpec((TILE_ROWS, width), lambda i, *_: (i, 0))
    return pl.pallas_call(
        table_kernel,
        grid_spec=pltpu.PrefetchScalarGridSpec(
            num_scalar_prefetch=2,
            grid=(pl.cdiv(height, TILE_ROWS),),
            in_specs=[
                tile,
                pl.BlockSpec(update.shape, lambda i, *_: (0, 0)),
                pl.BlockSpec(scale.shape, lambda i, *_: (0, 0)),
            ],
            out_specs=[tile, tile],
        ),
        out_shape=[
            jax.ShapeDtypeStruct((height, width), F32),
            jax.ShapeDtypeStruct((height, width), BF16),
        ],
        name="table_update",
    )(rows_at, starts, table, update, scale)


def norm_forward(values, gain_row, bias_row):
    center = values - jnp.mean(values, -1, keepdims=True)
    spread = jnp.mean(center * center, -1, keepdims=True)
    inverse = lax.rsqrt(spread + NORM_EPSILON)
    unit = center * inverse
    return unit * gain_row + bias_row, (unit, inverse)


def norm_backward(d_out, kept, gain_row):
    unit, inverse = kept
    scaled = d_out * gain_row
    d_in = inverse * (
        scaled - jnp.mean(scaled, -1, keepdims=True) - unit * jnp.mean(scaled * unit, -1, keepdims=True)
    )
    return d_in, jnp.sum(d_out * unit, 0), jnp.sum(d_out, 0)


def gelu_and_slope(values):
    normal = 0.5 + 0.5 * lax.erf(values * math.sqrt(0.5))
    slope = normal + values * (jnp.exp(-0.5 * values * values) * (1.0 / math.sqrt(2.0 * math.pi)))
    return values * normal, slope


def exact(left, right, dims=CONTRACT_IN):
    return lax.dot_general(left, right, dims, precision=EXACT_PRECISION, preferred_element_type=F32)


def contrast_kernel(scale_ref, pooled_ref, head_ref, d_pooled_ref, d_projected_ref, loss_ref):
    projected = exact(pooled_ref[...], head_ref[...])
    inverse = lax.rsqrt(jnp.sum(projected * projected, -1, keepdims=True) + UNIT_EPSILON)
    units = projected * inverse
    scale = jnp.exp(jnp.full((1, 1), scale_ref[0], F32))
    logits = scale * exact(units, units, CONTRACT_COLS)
    row = lax.broadcasted_iota(jnp.int32, logits.shape, 0)
    col = lax.broadcasted_iota(jnp.int32, logits.shape, 1)
    used = (row % 2 == 0) & (col % 2 == 1)
    pairs = used & (col == row + 1)
    total = jnp.zeros((1, 1), F32)
    d_logits = jnp.where(pairs, -1.0, 0.0)
    for axis in (1, 0):
        seen = jnp.where(used, logits, -1e30)
        peak = jnp.max(seen, axis, keepdims=True)
        raised = jnp.where(used, jnp.exp(seen - peak), 0.0)
        sums = jnp.sum(raised, axis, keepdims=True)
        safe = jnp.where(sums > 0.0, sums, 1.0)
        d_logits += 0.5 * raised / safe
        logs = jnp.where(sums > 0.0, peak + jnp.log(safe), 0.0)
        total += 0.5 * jnp.sum(jnp.sum(logs, 1, keepdims=True), 0, keepdims=True)
    matched = jnp.where(pairs, logits, 0.0)
    total -= jnp.sum(jnp.sum(matched, 1, keepdims=True), 0, keepdims=True)
    weighted = jnp.where(used, d_logits * logits, 0.0)
    d_scale = jnp.sum(jnp.sum(weighted, 1, keepdims=True), 0, keepdims=True)
    d_units = scale * (exact(d_logits, units) + exact(d_logits, units, CONTRACT_ROWS))
    along = jnp.sum(projected * d_units, -1, keepdims=True)
    d_projected = inverse * d_units - projected * (inverse * inverse * inverse * along)
    d_projected_ref[...] = d_projected
    d_pooled_ref[...] = exact(d_projected, head_ref[...], CONTRACT_COLS)
    lane = lax.broadcasted_iota(jnp.int32, (8, 128), 1)
    loss_ref[...] = jnp.where(lane == 0, total, jnp.where(lane == 1, d_scale, 0.0))


def contrast(pooled, head_weight, log_scale):
    vmem = pl.BlockSpec(memory_space=pltpu.VMEM)
    like = jax.ShapeDtypeStruct(pooled.shape, F32)
    return pl.pallas_call(
        contrast_kernel,
        in_specs=[pl.BlockSpec(memory_space=pltpu.SMEM), vmem, vmem],
        out_specs=[vmem] * 3,
        out_shape=[like, like, jax.ShapeDtypeStruct((8, 128), F32)],
        name="contrast",
    )(log_scale.reshape(1), pooled, head_weight)


def factored_step(gradient, rows_old, cols_old):
    square = gradient * gradient
    rows_new = DECAY_RATE * rows_old + (1.0 - DECAY_RATE) * (jnp.mean(square, 1) + FLOOR_SQUARE)
    cols_new = DECAY_RATE * cols_old + (1.0 - DECAY_RATE) * (jnp.mean(square, 0) + FLOOR_SQUARE)
    estimate = rows_new[:, None] * cols_new[None, :] / jnp.mean(rows_new)
    return (gradient * lax.rsqrt(estimate), rows_new, cols_new)


def plain_step(gradient, moment_old):
    moment_new = DECAY_RATE * moment_old + (1.0 - DECAY_RATE) * (gradient * gradient + FLOOR_SQUARE)
    return (gradient * lax.rsqrt(moment_new), moment_new)


def apply_update(weight_matrix, update, square):
    spread = jnp.sqrt(jnp.mean(update * update))
    clip_factor = jnp.maximum(1.0, spread / CLIP_LIMIT)
    step_size = RELATIVE * jnp.maximum(FLOOR_SCALE, jnp.sqrt(square))
    return (weight_matrix - step_size * (update / clip_factor), spread)


def body(
    token_ids,
    seq_lengths,
    embedding,
    embed_rows,
    embed_cols,
    layers,
    layer_rows,
    layer_cols,
    head_weight,
    head_rows,
    head_cols,
    positions,
    pos_rows,
    pos_cols,
    norm_vectors,
    vector_moment,
    log_scale,
    scale_moment,
):
    outer = lax.axis_size("dp")
    inner = lax.axis_size("fsdp")
    devices = outer * inner
    outer_index = lax.axis_index("dp")
    inner_index = lax.axis_index("fsdp")
    seq_count = token_ids.shape[0]
    slots = seq_count * MAXLEN
    cap = slots // outer
    shard_rows, shard_cols = embedding.shape
    local_rows, local_cols = layers.shape[1], layers.shape[2]
    gather_orders = bit_orders(outer)
    scatter_orders = [order[::-1] for order in gather_orders]
    block_orders = sum_orders(outer)
    inner_order = list(range(bit_count(inner)))

    flat = token_ids.reshape(slots)
    owners = flat // shard_rows
    offsets = flat - owners * shard_rows
    hot = owners[:, None] == jnp.arange(outer, dtype=jnp.int32)[None, :]
    counting = jnp.arange(slots, dtype=jnp.int32)
    before = dot((counting[:, None] >= counting[None, :]).astype(BF16), hot.astype(BF16))
    rank = jnp.sum(jnp.where(hot, before, 0.0), 1).astype(jnp.int32) - 1
    bucket = owners * cap + rank
    outgoing = jnp.sum(jnp.where(counting[:, None] == bucket[None, :], offsets[None, :], 0), 1)
    asked = lax.all_to_all(outgoing.reshape(outer, cap), "dp", 0, 0, tiled=True)
    wanted = jnp.stack([asked] + fsdp_others(asked, inner), 1).reshape(-1)
    entries = wanted.shape[0]

    wanted, forward_vectors, forward_positions, lengths = lax.optimization_barrier(
        (wanted, norm_vectors, positions, seq_lengths.astype(jnp.int32))
    )

    old_rows_mean = jnp.mean(embed_rows)

    low_layers = layers[0].astype(BF16)
    width = local_cols // COLORS
    gathered = []
    for color in range(COLORS):
        piece = low_layers[:, color * width : (color + 1) * width]
        whole = gather_bits(piece, "dp", outer, gather_orders[color]).reshape(MODEL_WIDTH, width)
        gathered.append(gather_list(whole, "fsdp", inner))
    pieces = [gathered[color][f] for f in range(inner) for color in range(COLORS)]
    group = PIECE // width
    weights = [
        pieces[k] if group == 1 else jnp.concatenate(pieces[k * group : (k + 1) * group], 1)
        for k in range(COLUMNS // PIECE)
    ]
    w_qk, w_vo, w_up, w_down = weights[0], weights[1], weights[2:4], weights[4:6]
    w_v, w_o = w_vo[:, :MODEL_WIDTH], w_vo[:, MODEL_WIDTH:]

    looked = take_rows(wanted, embedding).reshape(outer, inner, cap, shard_cols)
    looked, *early = lax.optimization_barrier((looked, head_weight, positions, norm_vectors, layers[0]))
    replies = lax.all_to_all(looked, "dp", 0, 0, tiled=True)
    head_square, pos_square, vector_square = (jnp.mean(weight * weight) for weight in early[:3])
    layer_column_squares = jnp.sum(early[3] * early[3], 0)
    own_part = replies[:, 0].reshape(slots, shard_cols)
    other_parts = [swap_by(replies[:, d].reshape(slots, shard_cols), "fsdp", inner, d) for d in range(1, inner)]
    rows_low = in_order([own_part] + other_parts, inner, 1)
    token_rows = dot((bucket[:, None] == counting[None, :]).astype(BF16), rows_low)

    embedded = (token_rows.reshape(seq_count, MAXLEN, MODEL_WIDTH) + forward_positions[None]).reshape(slots, MODEL_WIDTH)
    vectors = forward_vectors[2 : 2 + PER_LAYER]
    bias_q, bias_v, bias_o, bias_d, gain_one, bias_one, gain_two, bias_two = (vectors[k] for k in range(8))
    bias_up = vectors[8:].reshape(2, PIECE)
    hidden, kept_zero = norm_forward(embedded, forward_vectors[0], forward_vectors[1])
    hidden_low = hidden.astype(BF16)
    qk = (dot(hidden_low, w_qk) + jnp.concatenate([bias_q, jnp.zeros_like(bias_q)])).astype(BF16)
    v = (dot(hidden_low, w_v) + bias_v).astype(BF16)
    attended = attend(lengths, qk, v)
    first, kept_one = norm_forward(hidden + (dot(attended, w_o) + bias_o), gain_one, bias_one)
    first_low = first.astype(BF16)
    active, slopes = [], []
    for k in range(2):
        value, slope = gelu_and_slope(dot(first_low, w_up[k]) + bias_up[k])
        active.append(value.astype(BF16))
        slopes.append(slope)
    downward = dot(active[0], w_down[0], CONTRACT_COLS) + dot(active[1], w_down[1], CONTRACT_COLS) + bias_d
    final, kept_two = norm_forward(first + downward, gain_two, bias_two)

    valid = (jnp.arange(MAXLEN)[None, :] < lengths[:, None]).astype(F32)
    lengths_float = lengths.astype(F32)[:, None]
    pooled = jnp.sum(final.reshape(seq_count, MAXLEN, MODEL_WIDTH) * valid[:, :, None], 1) / lengths_float
    all_pooled = everyone(pooled, BOTH, devices).reshape(devices * seq_count, MODEL_WIDTH)
    d_all_pooled, d_projected, loss_out = contrast(all_pooled, head_weight, log_scale)
    loss_value, grad_scale = loss_out[0, 0], loss_out[0, 1]
    device_index = outer_index * inner + inner_index
    d_pooled = lax.dynamic_slice_in_dim(d_all_pooled, device_index * seq_count, seq_count, 0)
    d_final = ((d_pooled / lengths_float)[:, None, :] * valid[:, :, None]).reshape(slots, MODEL_WIDTH)

    def columns_sum(make, whole):
        if inner != 2:
            return scatter_bits(whole(), "fsdp", inner, inner_order[::-1], 1)
        sent = swap(make(1 - inner_index).astype(BF16), "fsdp", 2, 0)
        return make(inner_index) + sent.astype(F32)

    def rows_sum(values, order):
        return scatter_bits(values, "dp", outer, order, 0)

    def of_two(half, pair):
        return jnp.where(half == 0, pair[0], pair[1])

    def half_columns(half, values):
        return lax.dynamic_slice_in_dim(values, half * (values.shape[1] // 2), values.shape[1] // 2, 1)

    d_two, d_gain_two, d_bias_two = norm_backward(d_final, kept_two, gain_two)
    d_two_low = d_two.astype(BF16)
    part_down = columns_sum(
        lambda half: dot(d_two_low, of_two(half, active), CONTRACT_ROWS),
        lambda: jnp.concatenate([dot(d_two_low, active[k], CONTRACT_ROWS) for k in range(2)], 1),
    )
    sum_down = rows_sum(part_down, block_orders[0])
    d_ups = [slopes[k] * dot(d_two_low, w_down[k]) for k in range(2)]
    d_up_lows = [d_up.astype(BF16) for d_up in d_ups]
    part_up = columns_sum(
        lambda half: dot(first_low, of_two(half, d_up_lows), CONTRACT_ROWS),
        lambda: jnp.concatenate([dot(first_low, d_up_lows[k], CONTRACT_ROWS) for k in range(2)], 1),
    )
    sum_up = rows_sum(part_up, block_orders[1])
    d_first = d_two + dot(d_up_lows[0], w_up[0], CONTRACT_COLS) + dot(d_up_lows[1], w_up[1], CONTRACT_COLS)
    d_one, d_gain_one, d_bias_one = norm_backward(d_first, kept_one, gain_one)
    d_one_low = d_one.astype(BF16)
    d_attended = dot(d_one_low, w_o, CONTRACT_COLS).astype(BF16)
    part_out = columns_sum(
        lambda half: dot(attended, half_columns(half, d_one_low), CONTRACT_ROWS),
        lambda: dot(attended, d_one_low, CONTRACT_ROWS),
    )
    sum_out = rows_sum(part_out, block_orders[2])
    d_heads = ()
    for seq in range(seq_count):
        d_heads = attend_back(seq, lengths, qk, v, d_attended, d_heads)
    d_q, d_k, d_v, d_sums = d_heads
    d_hidden = (
        d_one
        + dot(d_q, w_qk[:, :MODEL_WIDTH], CONTRACT_COLS)
        + dot(d_k, w_qk[:, MODEL_WIDTH:], CONTRACT_COLS)
        + dot(d_v, w_v, CONTRACT_COLS)
    )
    d_embedded, d_gain_zero, d_bias_zero = norm_backward(d_hidden, kept_zero, forward_vectors[0])

    d_tokens = d_embedded.astype(BF16)
    back_rows = dot((counting[:, None] == bucket[None, :]).astype(BF16), d_tokens).astype(BF16)
    parts = [
        lax.dynamic_slice_in_dim(back_rows, (inner_index ^ d) * shard_cols, shard_cols, 1) for d in range(inner)
    ]
    parts = parts[:1] + [swap_by(parts[d], "fsdp", inner, d) for d in range(1, inner)]
    back = jnp.concatenate([rows.reshape(outer, 1, cap, shard_cols) for rows in parts], 1)
    (
        back,
        d_embedded,
        d_q,
        d_k,
        d_v,
        embed_rows,
        embed_cols,
        layer_rows,
        layer_cols,
        layers,
        head_weight,
        head_rows,
        head_cols,
        positions,
        pos_rows,
        pos_cols,
        norm_vectors,
        vector_moment,
        all_pooled,
        d_projected,
    ) = lax.optimization_barrier(
        (
            back,
            d_embedded,
            d_q,
            d_k,
            d_v,
            embed_rows,
            embed_cols,
            layer_rows,
            layer_cols,
            layers,
            head_weight,
            head_rows,
            head_cols,
            positions,
            pos_rows,
            pos_cols,
            norm_vectors,
            vector_moment,
            all_pooled,
            d_projected,
        )
    )
    returned = lax.all_to_all(back, "dp", 0, 0, tiled=True).reshape(entries, shard_cols)

    head_sums = d_sums.reshape(seq_count, 8, MODEL_WIDTH).sum(0)
    d_bias_out, d_bias_down = jnp.sum(d_one, 0), jnp.sum(d_two, 0)
    d_bias_ups = [jnp.sum(d_up, 0) for d_up in d_ups]
    d_positions = jnp.sum(d_embedded.reshape(seq_count, MAXLEN, MODEL_WIDTH), 0)
    part = MODEL_WIDTH // inner
    part_positions = columns_sum(lambda half: half_columns(half, d_positions), lambda: d_positions)
    reduced = []
    for color, d_rows in enumerate((d_q, d_k, d_v)):
        block = columns_sum(
            lambda half: dot(hidden_low, half_columns(half, d_rows), CONTRACT_ROWS),
            lambda: dot(hidden_low, d_rows, CONTRACT_ROWS),
        ).reshape(outer, local_rows, part)
        if color == 0:
            block = jnp.concatenate([block, part_positions.reshape(outer, MAXLEN // outer, part)], 1)
        reduced.append(rows_sum(block, scatter_orders[color])[0])
    own_positions = reduced[0][local_rows:]
    reduced[0] = reduced[0][:local_rows]
    vector_rows = [
        d_gain_zero,
        d_bias_zero,
        head_sums[0],
        head_sums[1],
        d_bias_out,
        d_bias_down,
        d_gain_one,
        d_bias_one,
        d_gain_two,
        d_bias_two,
    ]
    for sums in d_bias_ups:
        vector_rows += [sums[k * MODEL_WIDTH : (k + 1) * MODEL_WIDTH] for k in range(PIECE // MODEL_WIDTH)]
    row_index = jnp.arange(len(vector_rows))[:, None]
    d_vectors = jnp.zeros((len(vector_rows), MODEL_WIDTH), F32)
    for k, row in enumerate(vector_rows):
        d_vectors = jnp.where(row_index == k, row[None, :], d_vectors)
    vector_share = d_vectors.size // devices

    def to_columns(values):
        whole = gather_list(values, "fsdp", inner)
        return lambda low, high: jnp.concatenate([piece[:, low:high] for piece in whole], 1)

    early = to_columns(jnp.concatenate([sum_out, sum_up, sum_down], 1))
    late = to_columns(jnp.concatenate(reduced, 1))
    cut = [0, part, part + FF // inner, part + 2 * FF // inner]
    full_grad = jnp.concatenate(
        [late(k * part, (k + 1) * part) for k in range(3)] + [early(cut[k], cut[k + 1]) for k in range(3)], 1
    )
    grad_layers = lax.dynamic_slice_in_dim(full_grad, inner_index * local_cols, local_cols, 1)

    entry = jnp.arange(entries, dtype=jnp.int32)
    goes_before = (wanted[None, :] < wanted[:, None]) | (
        (wanted[None, :] == wanted[:, None]) & (entry[None, :] < entry[:, None])
    )
    rank = jnp.sum(goes_before.astype(jnp.int32), 1)
    rows_at = jnp.sum(jnp.where(rank[None, :] == entry[:, None], wanted[None, :], 0), 1)
    is_first = jnp.concatenate([jnp.ones((1,), bool), rows_at[1:] != rows_at[:-1]]).astype(F32)
    tiles = -(-shard_rows // TILE_ROWS)
    starts = jnp.sum(
        (rows_at[None, :] < (jnp.arange(tiles + 1, dtype=jnp.int32) * TILE_ROWS)[:, None]).astype(jnp.int32), 1
    )
    lanes = 128
    high, low_digit = rows_at // lanes, rows_at % lanes
    digits = -(-shard_rows // lanes)
    high_hot = (jnp.arange(digits, dtype=jnp.int32)[:, None] == high[None, :]).astype(F32)
    low_hot = (low_digit[:, None] == jnp.arange(lanes, dtype=jnp.int32)[None, :]).astype(F32)
    own_rows_old = lax.dynamic_slice_in_dim(embed_rows, outer_index * shard_rows, shard_rows)
    dense_old = jnp.pad(own_rows_old, (0, digits * lanes - shard_rows)).reshape(digits, lanes)
    picked = lax.dot_general(high_hot, dense_old, CONTRACT_ROWS, precision=EXACT_PRECISION)
    entry_rows_old = jnp.sum(picked * low_hot, 1)
    embed_square = jnp.sum(embedding * embedding)

    grad_rows = dot((rows_at[:, None] == wanted[None, :]).astype(BF16), returned)
    row_part = jnp.sum(grad_rows * grad_rows, 1)
    row_sums = row_part
    for bit in inner_order:
        row_sums = row_sums + swap(row_sums, "fsdp", inner, bit)
    entry_rows = DECAY_RATE * entry_rows_old + (1.0 - DECAY_RATE) * (row_sums / MODEL_WIDTH + FLOOR_SQUARE)
    scaled_rows = grad_rows * lax.rsqrt(entry_rows)[:, None]
    col_part = jnp.sum(grad_rows * grad_rows * is_first[:, None], 0)
    scaled_part = jnp.sum(scaled_rows * scaled_rows * is_first[:, None], 0)
    common = jnp.concatenate([col_part, scaled_part, jnp.sum(row_part * is_first)[None], embed_square[None]])
    payload = jnp.concatenate(
        [
            jnp.broadcast_to(common[None], (devices, common.size)),
            d_vectors.reshape(devices, vector_share),
        ],
        1,
    )
    payload = jnp.pad(payload, ((0, 0), (0, -payload.shape[1] % 1024))).reshape(devices, -1, 128)
    stats = lax.all_to_all(payload, BOTH, 0, 0, tiled=True).reshape(devices, -1)
    own_vectors = jnp.sum(stats[:, common.size : common.size + vector_share], 0)
    embed_stats = own_vectors
    stats = stats[:, : common.size].reshape(outer, inner, common.size).sum(0)
    embed_col_sum = stats[:, :shard_cols].reshape(-1)
    scaled_sum = stats[:, shard_cols : 2 * shard_cols].reshape(-1)
    embed_total, embed_squares = jnp.sum(stats[:, -2]), jnp.sum(stats[:, -1])
    embed_cols_new = DECAY_RATE * embed_cols + (1.0 - DECAY_RATE) * (embed_col_sum / VOCAB + FLOOR_SQUARE)
    rows_mean = DECAY_RATE * old_rows_mean + (1.0 - DECAY_RATE) * (
        embed_total / MODEL_WIDTH / VOCAB + FLOOR_SQUARE
    )
    count = float(VOCAB * MODEL_WIDTH)
    embed_spread = jnp.sqrt(jnp.sum(scaled_sum * (rows_mean / embed_cols_new)) / count)
    embed_step = RELATIVE * jnp.maximum(FLOOR_SCALE, jnp.sqrt(embed_squares / count))
    embed_scale = embed_step / jnp.maximum(1.0, embed_spread / CLIP_LIMIT)
    own_cols = lax.dynamic_slice_in_dim(embed_cols_new, inner_index * shard_cols, shard_cols)
    col_scale = embed_scale * lax.rsqrt(own_cols / rows_mean)
    embedding_new, embedding_copy = table_update(rows_at, starts, embedding, scaled_rows, col_scale[None])
    dense_rows = jnp.dot(
        high_hot, low_hot * (row_sums * is_first)[:, None], precision=EXACT_PRECISION
    ).reshape(-1)

    unit = math.gcd(local_cols, MODEL_WIDTH)
    groups = local_cols // unit
    bounds = [0, 1, 2, 3, 4, 4 + FF // MODEL_WIDTH, 4 + 2 * FF // MODEL_WIDTH]
    bounds = [b * (MODEL_WIDTH // unit) for b in bounds]
    widths = jnp.array([MODEL_WIDTH] * 4 + [FF] * 2, F32)

    def by_block(values):
        return jnp.stack([jnp.sum(values[..., bounds[b] : bounds[b + 1]], -1) for b in range(6)], -1)

    def by_group(values):
        return jnp.stack([jnp.sum(values[..., g * unit : (g + 1) * unit], -1) for g in range(groups)], -1)

    def own_groups(block_values):
        per_group = jnp.stack([block_values[..., b] for b in range(6) for _ in range(bounds[b + 1] - bounds[b])], -1)
        return lax.dynamic_slice_in_dim(per_group, inner_index * groups, groups, per_group.ndim - 1)

    def over_columns(group_values, columns):
        return jnp.concatenate(
            [jnp.broadcast_to(group_values[:, g : g + 1], (group_values.shape[0], unit)) for g in range(columns)], 1
        )

    layer_square = grad_layers * grad_layers
    row_groups = by_group(layer_square)
    all_groups = jnp.concatenate(gather_list(row_groups, "fsdp", inner), 1)
    own_row_sums = by_block(all_groups)
    own_rows_before = lax.dynamic_slice_in_dim(layer_rows[0], outer_index * local_rows, local_rows, 1)
    own_layer_rows = DECAY_RATE * own_rows_before.T + (1.0 - DECAY_RATE) * (
        own_row_sums / widths[None, :] + FLOOR_SQUARE
    )
    scaled_grad = grad_layers * over_columns(lax.rsqrt(own_groups(own_layer_rows)), groups)
    weight_groups = by_group(layer_column_squares)
    lead = 1024
    payload = jnp.concatenate(
        [
            padded(jnp.concatenate([own_row_sums.reshape(-1), weight_groups]), lead),
            jnp.sum(layer_square, 0),
            jnp.sum(scaled_grad * scaled_grad, 0),
        ]
    )
    payload = jnp.concatenate([payload.reshape(-1, 128), padded(own_positions.reshape(-1), 1024).reshape(-1, 128)], 0)
    payload, _ = lax.optimization_barrier((payload, embed_stats))
    stats_rows = (lead + 2 * local_cols) // 128
    stats = everyone(payload, "dp", outer)
    stats, pos_stats = stats[:, :stats_rows].reshape(outer, -1), stats[:, stats_rows:].reshape(outer, -1)
    pos_stats = pos_stats[:, : own_positions.size].reshape(MAXLEN, part)
    grad_pos = jnp.concatenate(gather_list(pos_stats, "fsdp", inner), 1)
    row_stats = stats[:, : local_rows * 6].reshape(MODEL_WIDTH, 6)
    layer_rows_new = DECAY_RATE * layer_rows[0] + (1.0 - DECAY_RATE) * (
        row_stats.T / widths[:, None] + FLOOR_SQUARE
    )
    col_stats = jnp.sum(stats[:, local_rows * 6 :], 0)
    own_weight_groups, col_stats = col_stats[:groups], col_stats[lead - local_rows * 6 :]
    own_cols_before = lax.dynamic_slice_in_dim(layer_cols[0], inner_index * local_cols, local_cols, 0)
    own_layer_cols = DECAY_RATE * own_cols_before + (1.0 - DECAY_RATE) * (
        col_stats[:local_cols] / MODEL_WIDTH + FLOOR_SQUARE
    )
    rows_means = jnp.mean(layer_rows_new, -1)
    ratio = col_stats[local_cols:] / own_layer_cols
    own_share = jnp.stack([jnp.sum(ratio[g * unit : (g + 1) * unit]) for g in range(groups)])
    sums_row = jnp.pad(jnp.stack([own_share, own_weight_groups]), ((0, 0), (0, 128 - groups)))
    share_rows = jnp.concatenate([own_layer_cols.reshape(-1, 128), sums_row], 0)
    shares = gather_list(share_rows, "fsdp", inner)
    layer_cols_new = jnp.concatenate([values[:-2] for values in shares], 0).reshape(-1)
    update_groups = jnp.concatenate([values[-2, :groups] for values in shares])
    weight_groups = jnp.concatenate([values[-1, :groups] for values in shares])
    counts = MODEL_WIDTH * widths
    spreads = jnp.sqrt(by_block(update_groups) * rows_means / counts)
    layer_scale = (
        RELATIVE
        * jnp.maximum(FLOOR_SCALE, jnp.sqrt(by_block(weight_groups) / counts))
        / jnp.maximum(1.0, spreads / CLIP_LIMIT)
    )
    group_scale = own_groups(layer_scale * jnp.sqrt(rows_means))
    col_factor = (lax.rsqrt(own_layer_cols).reshape(groups, unit) * group_scale[:, None]).reshape(1, local_cols)
    layers_new = layers[0] - scaled_grad * col_factor

    own_dense = dense_rows[:shard_rows]
    share = -(-shard_rows // inner)
    dense_pad = jnp.pad(own_dense, (0, share * inner - shard_rows))
    own_share = lax.dynamic_slice_in_dim(dense_pad, inner_index * share, share)
    flat_part = padded(jnp.concatenate([own_vectors, own_share]), 1024).reshape(-1, 128)
    payload, _ = lax.optimization_barrier((flat_part, stats))
    spread = everyone(payload, "dp", outer)
    spread = gather_list(spread, "fsdp", inner)
    flats = [values.reshape(outer, -1) for values in spread]
    grad_vectors = jnp.stack([values[:, :vector_share] for values in flats], 1).reshape(norm_vectors.shape)
    embed_row_sum = jnp.concatenate([values[:, vector_share : vector_share + share] for values in flats], 1)
    embed_row_sum = embed_row_sum[:, :shard_rows].reshape(-1)
    embed_rows_new = DECAY_RATE * embed_rows + (1.0 - DECAY_RATE) * (embed_row_sum / MODEL_WIDTH + FLOOR_SQUARE)

    grad_head = lax.dot_general(all_pooled, d_projected, CONTRACT_ROWS, precision=EXACT_PRECISION)
    head_update, head_rows_new, head_cols_new = factored_step(grad_head, head_rows, head_cols)
    head_new, head_spread = apply_update(head_weight, head_update, head_square)
    pos_update, pos_rows_new, pos_cols_new = factored_step(grad_pos, pos_rows, pos_cols)
    positions_new, pos_spread = apply_update(positions, pos_update, pos_square)
    vector_update, vector_moment_new = plain_step(grad_vectors, vector_moment)
    vectors_new, vector_spread = apply_update(norm_vectors, vector_update, vector_square)
    scale_update, scale_moment_new = plain_step(grad_scale, scale_moment)
    log_scale_new, scale_spread = apply_update(log_scale, scale_update, log_scale * log_scale)
    singles = (embed_spread, head_spread, pos_spread, vector_spread, scale_spread)
    update_rms = jnp.pad(spreads, (len(singles), 0))
    for k, single in enumerate(singles):
        update_rms = jnp.where(jnp.arange(update_rms.shape[0]) == k, single, update_rms)
    return (
        loss_value,
        embedding_new,
        embed_rows_new,
        embed_cols_new,
        embedding_copy,
        layers_new[None],
        layer_rows_new[None],
        layer_cols_new[None],
        layers_new.astype(BF16)[None],
        head_new,
        head_rows_new,
        head_cols_new,
        positions_new,
        pos_rows_new,
        pos_cols_new,
        vectors_new,
        vector_moment_new,
        log_scale_new,
        scale_moment_new,
        update_rms,
    )


def solution(mesh):
    split = P("dp", "fsdp")
    layer_split = P(None, "dp", "fsdp")
    whole = P()
    return jax.shard_map(
        body,
        mesh=mesh,
        in_specs=(P(BOTH, None), P(BOTH), split, whole, whole, layer_split) + (whole,) * 12,
        out_specs=(whole, split, whole, whole, split, layer_split, whole, whole, layer_split) + (whole,) * 11,
        check_vma=False,
    )
```
